256 devices in a mesh: pb: 64 (over x, z_hi, y), ka: 4 (over z_lo, core).
Axes of the slice: x: 4, y: 4, z: 8 (z_hi: 4, z_lo: 2; z = z_hi * 2 + z_lo), core: 2. Of those that a mesh axis runs over, the one named last changes fastest.
Arguments:
- coupling: bfloat16 [2, 320, 4800, 320], P(None, 'ka', 'pb'), may hold values from -0.019897461 to 0.019897461
- kpoints: int32 [3, 16], replicated, may hold values from 0 to 99
- qpoints: int32 [3, 256], replicated, may hold values from 0 to 99
- electron_cells: int32 [3, 320], replicated, may hold values from -6 to 6
- phonon_cells: int32 [3, 320], replicated, may hold values from -6 to 6
- phonon_modes: bfloat16 [256, 2, 120, 120], P('pb'), may hold values from -0.375 to 0.375
- band_vectors: bfloat16 [256, 16, 2, 40, 40], P('pb', 'ka'), may hold values from -0.625 to 0.625
- energies_kq: float32 [256, 16, 40], P('pb', 'ka'), may hold values from -0.5 to 0.5
- occupations_kq: float32 [256, 16, 40], P('pb', 'ka'), may hold values from 0 to 1
- energy_k: float32 [16], P('ka'), may hold values from -0.5 to 0.5
- occupation_k: float32 [16], P('ka'), may hold values from 0 to 1
- frequencies: float32 [256, 120], P('pb'), may hold values from 0.02 to 0.2
- bose_factors: float32 [256, 120], P('pb'), may hold values from 0.1 to 5
Outputs:
- electron_width: float32 [16, 120], P('ka')
- phonon_width: float32 [256, 120], P('pb')
The draws below stay inside these ranges and needn't reach their ends.
All inputs are finite; a program needn't handle non-finite values.
Results may differ from the reference program's by a relative error of at most 0.0066.
Values may be sent and summed in bfloat16 or wider, within the bound.
No kernel may reach another device: no remote copies, remote signals or barrier semaphores. Data moves between devices by JAX's collectives and lax.ppermute only.
A program may use at most 128 MiB of HBM per device.

```python
import math
import jax
import jax.numpy as jnp
from jax import lax

NB = 40
MODES = 120
CE = 320
CP = 320
NG = 100
QD = 4
PAIRS = 4800
KTOT = 16
QTOT = 256


def set_ends(result, key, least, top_value):
    place = [jax.random.randint(jax.random.fold_in(key, axis), (), 0, length) for axis, length in enumerate(result.shape)]
    main_axis = result.shape.index(max(result.shape))
    beside = place[:main_axis] + [(place[main_axis] + 1) % result.shape[main_axis]] + place[main_axis + 1:]
    return result.at[tuple(place)].set(least).at[tuple(beside)].set(top_value)


def level_of(key, extent, shards, smallest, high):
    gain = 1.0
    for position, shards_of in shards:
        steps = jax.random.uniform(jax.random.fold_in(jax.random.fold_in(key, 6), position), (shards_of,), jnp.float32, smallest / len(shards), high / len(shards))
        gain = gain * jnp.repeat(jnp.exp(steps), extent[position] // shards_of).reshape((-1,) + (1,) * (len(extent) - 1 - position))
    return gain


def centred(own_key, dims, scale, limit, split=(), held_as=jnp.bfloat16):
    array = scale * jax.random.normal(own_key, dims, jnp.float32)
    if split:
        array = array * level_of(own_key, dims, split, -0.22, 0.18)
    return jnp.clip(array, -limit, limit).astype(held_as)


def setup_inputs(seed: int = 0) -> dict:
    seeds = jax.random.split(jax.random.key(seed), 14)
    coupling = centred(seeds[0], (2, CE, PAIRS, CP), 0.003125, 0.019897461, ((1, 4), (2, 64)))
    kpoints = set_ends(jax.random.randint(seeds[1], (3, KTOT), 0, NG), jax.random.fold_in(seeds[1], 1), 0, NG - 1).astype(jnp.int32)
    qpoints = set_ends(jax.random.randint(seeds[2], (3, QTOT), 0, NG), jax.random.fold_in(seeds[2], 1), 0, NG - 1).astype(jnp.int32)
    electron_cells = set_ends(jax.random.randint(seeds[3], (3, CE), -6, 7), jax.random.fold_in(seeds[3], 1), -6, 6).astype(jnp.int32)
    phonon_cells = set_ends(jax.random.randint(seeds[4], (3, CP), -6, 7), jax.random.fold_in(seeds[4], 1), -6, 6).astype(jnp.int32)
    phonon_modes = centred(seeds[5], (QTOT, 2, MODES, MODES), (2 * MODES) ** -0.5, 0.375, ((0, 64),))
    band_vectors = centred(seeds[6], (QTOT, KTOT, 2, NB, NB), (2 * NB) ** -0.5, 0.625, ((0, 64), (1, 4)))
    energies_kq = jnp.clip(jax.random.uniform(seeds[7], (QTOT, KTOT, NB), jnp.float32, -0.5, 0.5) * level_of(seeds[7], (QTOT, KTOT, NB), ((0, 64), (1, 4)), -0.4, 0.0), -0.5, 0.5)
    occupations_kq = jnp.clip(1.0 * jax.random.uniform(seeds[8], (QTOT, KTOT, NB), jnp.float32) ** level_of(seeds[8], (QTOT, KTOT, NB), ((0, 64), (1, 4)), -0.2, 0.2), 0.0, 1.0)
    energy_k = jnp.clip(jax.random.uniform(seeds[9], (KTOT,), jnp.float32, -0.5, 0.5) * level_of(seeds[9], (KTOT,), ((0, 4),), -0.4, 0.0), -0.5, 0.5)
    occupation_k = jnp.clip(1.0 * jax.random.uniform(seeds[10], (KTOT,), jnp.float32) ** level_of(seeds[10], (KTOT,), ((0, 4),), -0.2, 0.2), 0.0, 1.0)
    frequencies = jnp.clip(jnp.exp(math.log(0.2) - 2.3025851 * jax.random.uniform(seeds[11], (QTOT, MODES), jnp.float32) ** level_of(seeds[11], (QTOT, MODES), ((0, 64),), -0.2, 0.2)), 0.02, 0.2)
    bose_factors = jnp.clip(jnp.exp(math.log(5.0) - 3.912023 * jax.random.uniform(seeds[12], (QTOT, MODES), jnp.float32) ** level_of(seeds[12], (QTOT, MODES), ((0, 64),), -0.2, 0.2)), 0.1, 5.0)
    return {"coupling": coupling, "kpoints": kpoints, "qpoints": qpoints, "electron_cells": electron_cells, "phonon_cells": phonon_cells, "phonon_modes": phonon_modes, "band_vectors": band_vectors, "energies_kq": energies_kq, "occupations_kq": occupations_kq, "energy_k": energy_k, "occupation_k": occupation_k, "frequencies": frequencies, "bose_factors": bose_factors}


smearing = 0.05

def phase_table(points, cells):
    product = points[0][:, None] * cells[0][None, :] + points[1][:, None] * cells[1][None, :] + points[2][:, None] * cells[2][None, :]
    angle = jnp.mod(product, NG).astype(jnp.float32) * (2.0 * math.pi / NG)
    return (jnp.cos(angle).astype(jnp.bfloat16), jnp.sin(angle).astype(jnp.bfloat16))

def gaussian(offset):
    return jnp.exp(-0.5 * (offset / smearing) ** 2) / (smearing * math.sqrt(2.0 * math.pi))

def contract_last(left, right):
    return lax.dot_general(left, right, (((1,), (1,)), ((), ())), preferred_element_type=jnp.float32)

def floated(form, left, right):
    return jnp.einsum(form, left.astype(jnp.float32), right.astype(jnp.float32))

def widths(bloch_real, bloch_imag, modes, vectors, levels, filled, energy_k, occupation_k, omega, bose):
    mode_real = modes[:, 0]
    mode_imag = modes[:, 1]
    moded_real = (floated('kqnm,qmv->kqnv', bloch_real, mode_real) - floated('kqnm,qmv->kqnv', bloch_imag, mode_imag)).astype(jnp.bfloat16)
    moded_imag = (floated('kqnm,qmv->kqnv', bloch_real, mode_imag) + floated('kqnm,qmv->kqnv', bloch_imag, mode_real)).astype(jnp.bfloat16)
    vector_real = vectors[:, :, 0]
    vector_imag = vectors[:, :, 1]
    band_real = floated('qknb,kqnv->kqbv', vector_real, moded_real) + floated('qknb,kqnv->kqbv', vector_imag, moded_imag)
    band_imag = floated('qknb,kqnv->kqbv', vector_real, moded_imag) - floated('qknb,kqnv->kqbv', vector_imag, moded_real)
    weight = band_real * band_real + band_imag * band_imag
    level_kq = jnp.transpose(levels, (1, 0, 2))[..., None]
    filled_kq = jnp.transpose(filled, (1, 0, 2))[..., None]
    offset = energy_k[:, None, None, None] - level_kq
    freq = omega[None, :, None, :]
    boson = bose[None, :, None, :]
    absorb = gaussian(offset + freq)
    emit = gaussian(offset - freq)
    electron = lax.optimization_barrier(jnp.sum(weight * ((boson + filled_kq) * absorb + (boson + 1.0 - filled_kq) * emit), axis=(1, 2)))
    phonon = lax.optimization_barrier(jnp.sum(weight * (occupation_k[:, None, None, None] - filled_kq) * absorb, axis=(0, 2)))
    return (electron, phonon)

def reference(coupling, kpoints, qpoints, electron_cells, phonon_cells, phonon_modes, band_vectors, energies_kq, occupations_kq, energy_k, occupation_k, frequencies, bose_factors):
    cos_k, sin_k = phase_table(kpoints, electron_cells)
    cos_q, sin_q = phase_table(qpoints, phonon_cells)
    real_flat = coupling[0].reshape(CE * PAIRS, CP)
    imag_flat = coupling[1].reshape(CE * PAIRS, CP)
    count = QTOT // QD

    def block_step(total, index):
        start = (index * QD).astype(jnp.int32)
        cos_block = lax.dynamic_slice_in_dim(cos_q, start, QD, 0)
        sin_block = lax.dynamic_slice_in_dim(sin_q, start, QD, 0)
        half_real = (contract_last(cos_block, real_flat) - contract_last(sin_block, imag_flat)).astype(jnp.bfloat16).reshape(QD, CE, PAIRS)
        half_imag = (contract_last(cos_block, imag_flat) + contract_last(sin_block, real_flat)).astype(jnp.bfloat16).reshape(QD, CE, PAIRS)
        bloch_real = (floated('kr,qrp->kqp', cos_k, half_real) - floated('kr,qrp->kqp', sin_k, half_imag)).astype(jnp.bfloat16)
        bloch_imag = (floated('kr,qrp->kqp', cos_k, half_imag) + floated('kr,qrp->kqp', sin_k, half_real)).astype(jnp.bfloat16)
        bloch_real = bloch_real.reshape(KTOT, QD, NB, MODES)
        bloch_imag = bloch_imag.reshape(KTOT, QD, NB, MODES)
        electron, phonon = widths(bloch_real, bloch_imag, lax.dynamic_slice_in_dim(phonon_modes, start, QD, 0), lax.dynamic_slice_in_dim(band_vectors, start, QD, 0), lax.dynamic_slice_in_dim(energies_kq, start, QD, 0), lax.dynamic_slice_in_dim(occupations_kq, start, QD, 0), energy_k, occupation_k, lax.dynamic_slice_in_dim(frequencies, start, QD, 0), lax.dynamic_slice_in_dim(bose_factors, start, QD, 0))
        return (total + electron / (QTOT * NB), phonon / (KTOT * NB))
    initial = jnp.zeros((KTOT, MODES), jnp.float32)
    electron_width, phonon_blocks = lax.scan(block_step, initial, jnp.arange(count, dtype=jnp.int32))
    return (electron_width, phonon_blocks.reshape(QTOT, MODES))
```

```python
import math

import jax
import jax.numpy as jnp
from jax import lax
from jax.experimental import pallas as pl
from jax.experimental.pallas import tpu as pltpu
from jax.sharding import PartitionSpec as P

NB = 40
MODES = 120
NG = 100
SMEARING = 0.05

STRIP = 16
LANES = 128
PARTS = 8


def whole_turn_cosine(ticks):
    rest = ticks - NG * jnp.floor((ticks + 0.5) * (1.0 / NG))
    y = (jnp.abs(rest - NG // 2) - NG // 4) * (2.0 * math.pi / NG)
    z = y * y
    series = -1.0 / 39916800.0
    for term in (1.0 / 362880.0, -1.0 / 5040.0, 1.0 / 120.0, -1.0 / 6.0, 1.0):
        series = series * z + term
    return y * series


def small_dot(left, right, dims):
    return lax.dot_general(left, right, (dims, ((), ())), preferred_element_type=jnp.float32)


def product_kernel(
    kpt_ref, qpt_ref, ecell_ref, pcell_ref, g_ref, send_ref, keep_ref, table, mixer, rows
):
    step = pl.program_id(0)
    q_total = qpt_ref.shape[1]
    cells = g_ref.shape[2]
    groups = kpt_ref.shape[1] // 4
    bf16 = jnp.bfloat16

    @pl.when(step == 0)
    def _():
        mine = lax.axis_index("ka")
        kpt = kpt_ref[...].astype(jnp.float32).astype(bf16)
        qpt = qpt_ref[...].astype(jnp.float32).astype(bf16)
        ecell = ecell_ref[...].astype(jnp.float32).astype(bf16)
        pcell = pcell_ref[...].astype(jnp.float32).astype(bf16)
        source = lax.broadcasted_iota(jnp.int32, (kpt.shape[1], PARTS * groups), 0)
        row = lax.broadcasted_iota(jnp.int32, (kpt.shape[1], PARTS * groups), 1)
        wanted = jnp.bitwise_xor(row // PARTS, mine) * 4 + row % 4
        k_rows = small_dot(kpt, (source == wanted).astype(jnp.float32).astype(bf16), ((1,), (0,)))
        source = lax.broadcasted_iota(jnp.int32, (ecell.shape[1], 2 * cells), 0)
        col = lax.broadcasted_iota(jnp.int32, (ecell.shape[1], 2 * cells), 1)
        wanted = mine * cells + jnp.where(col >= cells, col - cells, col)
        e_cols = small_dot(ecell, (source == wanted).astype(jnp.float32).astype(bf16), ((1,), (0,)))
        ticks = small_dot(k_rows.astype(bf16), e_cols.astype(bf16), ((0,), (0,)))
        row = lax.broadcasted_iota(jnp.int32, ticks.shape, 0)
        col = lax.broadcasted_iota(jnp.int32, ticks.shape, 1)
        imaginary = row % PARTS >= 4
        second = col >= cells
        turn = jnp.where(imaginary, jnp.where(second, 0.0, -25.0), jnp.where(second, 25.0, 0.0))
        mixer[...] = whole_turn_cosine(ticks + turn).astype(bf16)
        ticks = small_dot(qpt, pcell, ((0,), (0,)))
        table[0:q_total, :] = whole_turn_cosine(ticks).astype(bf16)
        table[q_total : 2 * q_total, :] = whole_turn_cosine(ticks - 25.0).astype(bf16)

    mix = mixer[...]
    for j in range(STRIP):
        both = jnp.concatenate([g_ref[0, j], g_ref[1, j]], axis=0)
        value = jnp.dot(mix, both, preferred_element_type=jnp.float32)
        for t in range(rows.shape[0]):
            tile = value[:, t * LANES : (t + 1) * LANES]
            if tile.shape[1] < LANES:
                blank = jnp.zeros((tile.shape[0], LANES - tile.shape[1]), jnp.float32)
                tile = jnp.concatenate([tile, blank], axis=1)
            rows[t, pl.ds(j, PARTS * groups, stride=STRIP), :] = tile

    @pl.when(step == pl.num_programs(0) - 1)
    def _():
        empty = jnp.zeros((PARTS * groups, LANES), jnp.float32)
        for j in range(75 % STRIP, STRIP):
            for t in range(rows.shape[0]):
                rows[t, pl.ds(j, PARTS * groups, stride=STRIP), :] = empty

    every = jnp.concatenate([rows[t] for t in range(rows.shape[0])], axis=1)
    every = every[:, : table.shape[1]].astype(bf16)
    turned = small_dot(table[...], every, ((1,), (1,)))
    lane = lax.broadcasted_iota(jnp.int32, (q_total, LANES), 1)
    sign = jnp.where(lane < LANES // 2, -1.0, 1.0)
    for ref, slot, group in ((send_ref, 0, 3), (send_ref, 1, 1), (keep_ref, 0, 2), (keep_ref, 1, 0)):
        straight = turned[:q_total, group * LANES : (group + 1) * LANES]
        crossed = turned[q_total:, group * LANES : (group + 1) * LANES]
        ref[slot] = (straight + sign * pltpu.roll(crossed, LANES // 2, 1)).astype(bf16)


def products(kpoints, qpoints, electron_cells, phonon_cells, coupling):
    parts, cells, pairs, phonons = coupling.shape
    k_total = kpoints.shape[1]
    q_total = qpoints.shape[1]
    steps = pl.cdiv(pairs, STRIP)
    by_pair = jnp.transpose(coupling, (0, 2, 1, 3))
    whole = lambda a: pl.BlockSpec(a.shape, lambda i: (0, 0))
    out = jax.ShapeDtypeStruct((2, q_total, steps * LANES), jnp.bfloat16)
    out_spec = pl.BlockSpec((2, q_total, LANES), lambda i: (0, 0, i))
    return pl.pallas_call(
        product_kernel,
        grid=(steps,),
        in_specs=[
            whole(kpoints),
            whole(qpoints),
            whole(electron_cells),
            whole(phonon_cells),
            pl.BlockSpec((parts, STRIP, cells, phonons), lambda i: (0, i, 0, 0)),
        ],
        out_specs=[out_spec, out_spec],
        out_shape=[out, out],
        scratch_shapes=[
            pltpu.VMEM((2 * q_total, phonons), jnp.bfloat16),
            pltpu.VMEM((2 * k_total, 2 * cells), jnp.bfloat16),
            pltpu.VMEM((pl.cdiv(phonons, LANES), 2 * k_total * STRIP, LANES), jnp.float32),
        ],
        compiler_params=pltpu.CompilerParams(vmem_limit_bytes=48 << 20),
    )(kpoints, qpoints, electron_cells, phonon_cells, by_pair)


def table_kernel(
    level_ref, filled_ref, omega_ref, bose_ref, vector_ref, ek_ref, ok_ref,
    absorb_ref, count_ref, turned_ref, pick_ref,
):
    f32 = jnp.float32
    points = level_ref.shape[0]
    q_local = omega_ref.shape[0]
    level = jnp.transpose(level_ref[...])
    filled = jnp.transpose(filled_ref[...])
    scale = 1.0 / (SMEARING * math.sqrt(2.0 * math.pi))
    electron_scale = scale / (256 * NB)
    phonon_scale = scale / (16 * NB)
    for i in range(points):
        q, k = divmod(i, points // q_local)
        offset = ek_ref[k] - level[:, i : i + 1]
        f = filled[:, i : i + 1]
        w = omega_ref[q : q + 1, :]
        n = bose_ref[q : q + 1, :]
        up = jnp.exp(-0.5 * ((offset + w) / SMEARING) ** 2)
        down = jnp.exp(-0.5 * ((offset - w) / SMEARING) ** 2)
        absorb_ref[i] = ((n + f) * up + (n + 1.0 - f) * down) * electron_scale
        count_ref[i] = (ok_ref[k] - f) * up * phonon_scale
        for part in range(2):
            turned_ref[i, part * NB : (part + 1) * NB, :] = jnp.transpose(
                vector_ref[i, part].astype(f32)
            ).astype(jnp.bfloat16)
    lane = lax.broadcasted_iota(jnp.int32, pick_ref.shape, 0)
    col = lax.broadcasted_iota(jnp.int32, pick_ref.shape, 1)
    place = col % LANES
    wanted = (place // STRIP) * LANES + (col // LANES) * STRIP + place % STRIP
    pick_ref[...] = (lane == wanted).astype(f32).astype(jnp.bfloat16)


def tables(levels, filled, frequencies, bose, vectors, energy_k, occupation_k, width):
    q_local, k_local, bands = levels.shape
    points = q_local * k_local
    modes = frequencies.shape[1]
    vmem = pl.BlockSpec(memory_space=pltpu.VMEM)
    smem = pl.BlockSpec(memory_space=pltpu.SMEM)
    weight = jax.ShapeDtypeStruct((points, bands, modes), jnp.float32)
    return pl.pallas_call(
        table_kernel,
        in_specs=[vmem] * 5 + [smem] * 2,
        out_specs=[vmem] * 4,
        out_shape=[
            weight,
            weight,
            jax.ShapeDtypeStruct((points, 2 * bands, bands), jnp.bfloat16),
            jax.ShapeDtypeStruct((width, PARTS * LANES), jnp.bfloat16),
        ],
        compiler_params=pltpu.CompilerParams(vmem_limit_bytes=48 << 20),
    )(
        levels.reshape(points, bands),
        filled.reshape(points, bands),
        frequencies,
        bose,
        vectors.reshape(points, 2, bands, bands),
        energy_k,
        occupation_k,
    )


def width_kernel(
    block_ref, modes_ref, turned_ref, absorb_ref, count_ref, pick_ref,
    electron_ref, phonon_ref, spread, cycle, moded,
):
    f32 = jnp.float32
    bf16 = jnp.bfloat16
    q_local = modes_ref.shape[0]
    k_local = PARTS // 2
    rows = block_ref.shape[0]
    per_source = 75
    depth = 80
    sources = rows // q_local
    phases = 8
    runs = sources // phases
    block = block_ref[...]
    for part in range(PARTS):
        spread[part] = jnp.dot(
            block, pick_ref[:, part * LANES : (part + 1) * LANES], preferred_element_type=f32
        )
    electron_ref[...] = jnp.zeros(electron_ref.shape, f32)
    for q in range(q_local):
        for part in range(2):
            m = modes_ref[q, part].astype(f32)
            cycle[0:MODES, part * LANES : part * LANES + MODES] = m
            cycle[MODES : 2 * MODES, part * LANES : part * LANES + MODES] = m
        sums = [None] * 5
        for phase in range(phases):
            start = (per_source * phase) % MODES
            first = (per_source * phase) // MODES
            left = jnp.concatenate(
                [
                    spread[part, pl.ds(phase * q_local + q, runs, stride=phases * q_local), :]
                    for part in range(PARTS)
                ],
                axis=0,
            )[:, :depth].astype(bf16)
            right = cycle[pl.ds(start, depth), :]
            at = lax.broadcasted_iota(jnp.int32, right.shape, 0)
            until = min(MODES - start, per_source)
            pieces = [(first, jnp.where(at < until, right, 0.0))]
            if until < per_source:
                pieces.append(
                    (first + 1, jnp.where((at >= until) & (at < per_source), right, 0.0))
                )
            for n, piece in pieces:
                value = jnp.dot(left, piece.astype(bf16), preferred_element_type=f32)
                sums[n] = value if sums[n] is None else sums[n] + value
        half = PARTS // 2 * runs
        for n in range(5):
            real = sums[n][:half, :LANES] - sums[n][half:, LANES:]
            imag = sums[n][:half, LANES:] + sums[n][half:, :LANES]
            for k in range(k_local):
                moded[k, 0, pl.ds(n, runs, stride=5), :] = real[k * runs : (k + 1) * runs]
                moded[k, 1, pl.ds(n, runs, stride=5), :] = imag[k * runs : (k + 1) * runs]
        phonon = None
        for k in range(k_local):
            i = q * k_local + k
            right = jnp.concatenate([moded[k, 0], moded[k, 1]], axis=1).astype(bf16)
            both = jnp.dot(turned_ref[i], right, preferred_element_type=f32)
            real = both[:NB, :MODES] + both[NB:, LANES : LANES + MODES]
            imag = both[:NB, LANES : LANES + MODES] - both[NB:, :MODES]
            weight = real * real + imag * imag
            electron_ref[k : k + 1, :] += jnp.sum(weight * absorb_ref[i], axis=0, keepdims=True)
            value = jnp.sum(weight * count_ref[i], axis=0, keepdims=True)
            phonon = value if phonon is None else phonon + value
        phonon_ref[q : q + 1, :] = phonon


def widths(block, phonon_modes, turned, absorb, count, pick):
    q_local, _, modes, _ = phonon_modes.shape
    rows = block.shape[0]
    vmem = pl.BlockSpec(memory_space=pltpu.VMEM)
    return pl.pallas_call(
        width_kernel,
        in_specs=[vmem] * 6,
        out_specs=[vmem] * 2,
        out_shape=[
            jax.ShapeDtypeStruct((PARTS // 2, modes), jnp.float32),
            jax.ShapeDtypeStruct((q_local, modes), jnp.float32),
        ],
        scratch_shapes=[
            pltpu.VMEM((PARTS, rows, LANES), jnp.float32),
            pltpu.VMEM((2 * modes, 2 * LANES), jnp.float32),
            pltpu.VMEM((PARTS // 2, 2, NB, LANES), jnp.float32),
        ],
        compiler_params=pltpu.CompilerParams(vmem_limit_bytes=48 << 20),
    )(block, phonon_modes, turned, absorb, count, pick)


def sent_to_all(shard, axis):
    count = lax.axis_size(axis)
    return lax.all_to_all(
        jnp.broadcast_to(shard[None], (count, *shard.shape)), axis, 0, 0, tiled=True
    )


def added(left, right):
    return (left.astype(jnp.float32) + right.astype(jnp.float32)).astype(jnp.bfloat16)


def on_device(
    coupling,
    kpoints,
    qpoints,
    electron_cells,
    phonon_cells,
    phonon_modes,
    band_vectors,
    energies_kq,
    occupations_kq,
    energy_k,
    occupation_k,
    frequencies,
    bose_factors,
):
    q_local = frequencies.shape[0]
    send, keep = products(kpoints, qpoints, electron_cells, phonon_cells, coupling)
    q_total, width = send.shape[1:]
    members = lax.axis_size("ka")
    beside = [(i, i ^ 1) for i in range(members)]
    across = [(i, i ^ 2) for i in range(members)]
    chip = added(keep, lax.ppermute(send, "ka", beside))
    own = added(chip[1], lax.ppermute(chip[0], "ka", across))
    absorb, count, turned, pick = tables(
        energies_kq,
        occupations_kq,
        frequencies,
        bose_factors,
        band_vectors,
        energy_k,
        occupation_k,
        width,
    )
    chunks = own.reshape(q_total // q_local, q_local, width)
    arrived = lax.all_to_all(chunks, "pb", 0, 0, tiled=True)
    electron, phonon = widths(
        arrived.reshape(q_total, width), phonon_modes, turned, absorb, count, pick
    )
    electron_width = sent_to_all(electron, "pb").sum(axis=0)
    phonon_width = sent_to_all(phonon, "ka").sum(axis=0)
    return (electron_width, phonon_width)


def solution(mesh):
    in_specs = (
        P(None, "ka", "pb", None),
        P(),
        P(),
        P(),
        P(),
        P("pb", None, None, None),
        P("pb", "ka", None, None, None),
        P("pb", "ka", None),
        P("pb", "ka", None),
        P("ka"),
        P("ka"),
        P("pb", None),
        P("pb", None),
    )
    out_specs = (P("ka", None), P("pb", None))
    return jax.shard_map(
        on_device, mesh=mesh, in_specs=in_specs, out_specs=out_specs, check_vma=False
    )
```

```python
import math

import jax
import jax.numpy as jnp
from jax import lax
from jax.experimental import pallas as pl
from jax.experimental.pallas import tpu as pltpu
from jax.sharding import PartitionSpec as P

NB = 40
MODES = 120
NG = 100
SMEARING = 0.05

STRIP = 16
LANES = 128
PARTS = 8


def whole_turn_cosine(ticks):
    rest = ticks - NG * jnp.floor((ticks + 0.5) * (1.0 / NG))
    y = (jnp.abs(rest - NG // 2) - NG // 4) * (2.0 * math.pi / NG)
    z = y * y
    series = -1.0 / 39916800.0
    for term in (1.0 / 362880.0, -1.0 / 5040.0, 1.0 / 120.0, -1.0 / 6.0, 1.0):
        series = series * z + term
    return y * series


def small_dot(left, right, dims):
    return lax.dot_general(left, right, (dims, ((), ())), preferred_element_type=jnp.float32)


def product_kernel(
    kpt_ref, qpt_ref, ecell_ref, pcell_ref, g_ref, send_ref, keep_ref, table, mixer, rows
):
    step = pl.program_id(0)
    q_total = qpt_ref.shape[1]
    cells = g_ref.shape[2]
    groups = kpt_ref.shape[1] // 4
    bf16 = jnp.bfloat16

    @pl.when(step == 0)
    def _():
        mine = lax.axis_index("ka")
        kpt = kpt_ref[...].astype(jnp.float32).astype(bf16)
        qpt = qpt_ref[...].astype(jnp.float32).astype(bf16)
        ecell = ecell_ref[...].astype(jnp.float32).astype(bf16)
        pcell = pcell_ref[...].astype(jnp.float32).astype(bf16)
        source = lax.broadcasted_iota(jnp.int32, (kpt.shape[1], PARTS * groups), 0)
        row = lax.broadcasted_iota(jnp.int32, (kpt.shape[1], PARTS * groups), 1)
        wanted = jnp.bitwise_xor(row // PARTS, mine) * 4 + row % 4
        k_rows = small_dot(kpt, (source == wanted).astype(jnp.float32).astype(bf16), ((1,), (0,)))
        source = lax.broadcasted_iota(jnp.int32, (ecell.shape[1], 2 * cells), 0)
        col = lax.broadcasted_iota(jnp.int32, (ecell.shape[1], 2 * cells), 1)
        wanted = mine * cells + jnp.where(col >= cells, col - cells, col)
        e_cols = small_dot(ecell, (source == wanted).astype(jnp.float32).astype(bf16), ((1,), (0,)))
        ticks = small_dot(k_rows.astype(bf16), e_cols.astype(bf16), ((0,), (0,)))
        row = lax.broadcasted_iota(jnp.int32, ticks.shape, 0)
        col = lax.broadcasted_iota(jnp.int32, ticks.shape, 1)
        imaginary = row % PARTS >= 4
        second = col >= cells
        turn = jnp.where(imaginary, jnp.where(second, 0.0, -25.0), jnp.where(second, 25.0, 0.0))
        mixer[...] = whole_turn_cosine(ticks + turn).astype(bf16)
        ticks = small_dot(qpt, pcell, ((0,), (0,)))
        table[0:q_total, :] = whole_turn_cosine(ticks).astype(bf16)
        table[q_total : 2 * q_total, :] = whole_turn_cosine(ticks - 25.0).astype(bf16)

    mix = mixer[...]
    for j in range(STRIP):
        both = jnp.concatenate([g_ref[0, j], g_ref[1, j]], axis=0)
        value = jnp.dot(mix, both, preferred_element_type=jnp.float32)
        for t in range(rows.shape[0]):
            tile = value[:, t * LANES : (t + 1) * LANES]
            if tile.shape[1] < LANES:
                blank = jnp.zeros((tile.shape[0], LANES - tile.shape[1]), jnp.float32)
                tile = jnp.concatenate([tile, blank], axis=1)
            rows[t, pl.ds(j, PARTS * groups, stride=STRIP), :] = tile

    @pl.when(step == pl.num_programs(0) - 1)
    def _():
        empty = jnp.zeros((PARTS * groups, LANES), jnp.float32)
        for j in range(75 % STRIP, STRIP):
            for t in range(rows.shape[0]):
                rows[t, pl.ds(j, PARTS * groups, stride=STRIP), :] = empty

    every = jnp.concatenate([rows[t] for t in range(rows.shape[0])], axis=1)
    every = every[:, : table.shape[1]].astype(bf16)
    turned = small_dot(table[...], every, ((1,), (1,)))
    lane = lax.broadcasted_iota(jnp.int32, (q_total, LANES), 1)
    sign = jnp.where(lane < LANES // 2, -1.0, 1.0)
    for ref, slot, group in ((send_ref, 0, 3), (send_ref, 1, 1), (keep_ref, 0, 2), (keep_ref, 1, 0)):
        straight = turned[:q_total, group * LANES : (group + 1) * LANES]
        crossed = turned[q_total:, group * LANES : (group + 1) * LANES]
        ref[slot] = (straight + sign * pltpu.roll(crossed, LANES // 2, 1)).astype(bf16)


def products(kpoints, qpoints, electron_cells, phonon_cells, coupling):
    parts, cells, pairs, phonons = coupling.shape
    k_total = kpoints.shape[1]
    q_total = qpoints.shape[1]
    steps = pl.cdiv(pairs, STRIP)
    by_pair = jnp.transpose(coupling, (0, 2, 1, 3))
    whole = lambda a: pl.BlockSpec(a.shape, lambda i: (0, 0))
    out = jax.ShapeDtypeStruct((2, q_total, steps * LANES), jnp.bfloat16)
    out_spec = pl.BlockSpec((2, q_total, LANES), lambda i: (0, 0, i))
    return pl.pallas_call(
        product_kernel,
        grid=(steps,),
        in_specs=[
            whole(kpoints),
            whole(qpoints),
            whole(electron_cells),
            whole(phonon_cells),
            pl.BlockSpec((parts, STRIP, cells, phonons), lambda i: (0, i, 0, 0)),
        ],
        out_specs=[out_spec, out_spec],
        out_shape=[out, out],
        scratch_shapes=[
            pltpu.VMEM((2 * q_total, phonons), jnp.bfloat16),
            pltpu.VMEM((2 * k_total, 2 * cells), jnp.bfloat16),
            pltpu.VMEM((pl.cdiv(phonons, LANES), 2 * k_total * STRIP, LANES), jnp.float32),
        ],
        compiler_params=pltpu.CompilerParams(vmem_limit_bytes=48 << 20),
    )(kpoints, qpoints, electron_cells, phonon_cells, by_pair)


def table_kernel(
    level_ref, filled_ref, omega_ref, bose_ref, vector_ref, ek_ref, ok_ref,
    absorb_ref, count_ref, turned_ref, pick_ref,
):
    f32 = jnp.float32
    points = level_ref.shape[0]
    q_local = omega_ref.shape[0]
    level = jnp.transpose(level_ref[...])
    filled = jnp.transpose(filled_ref[...])
    scale = 1.0 / (SMEARING * math.sqrt(2.0 * math.pi))
    electron_scale = scale / (256 * NB)
    phonon_scale = scale / (16 * NB)
    for i in range(points):
        q, k = divmod(i, points // q_local)
        offset = ek_ref[k] - level[:, i : i + 1]
        f = filled[:, i : i + 1]
        w = omega_ref[q : q + 1, :]
        n = bose_ref[q : q + 1, :]
        up = jnp.exp(-0.5 * ((offset + w) / SMEARING) ** 2)
        down = jnp.exp(-0.5 * ((offset - w) / SMEARING) ** 2)
        absorb_ref[i] = ((n + f) * up + (n + 1.0 - f) * down) * electron_scale
        count_ref[i] = (ok_ref[k] - f) * up * phonon_scale
        for part in range(2):
            turned_ref[i, part * NB : (part + 1) * NB, :] = jnp.transpose(
                vector_ref[i, part].astype(f32)
            ).astype(jnp.bfloat16)
    lane = lax.broadcasted_iota(jnp.int32, pick_ref.shape, 0)
    col = lax.broadcasted_iota(jnp.int32, pick_ref.shape, 1)
    place = col % LANES
    wanted = (place // STRIP) * LANES + (col // LANES) * STRIP + place % STRIP
    pick_ref[...] = (lane == wanted).astype(f32).astype(jnp.bfloat16)


def tables(levels, filled, frequencies, bose, vectors, energy_k, occupation_k, width):
    q_local, k_local, bands = levels.shape
    points = q_local * k_local
    modes = frequencies.shape[1]
    vmem = pl.BlockSpec(memory_space=pltpu.VMEM)
    smem = pl.BlockSpec(memory_space=pltpu.SMEM)
    weight = jax.ShapeDtypeStruct((points, bands, modes), jnp.float32)
    return pl.pallas_call(
        table_kernel,
        in_specs=[vmem] * 5 + [smem] * 2,
        out_specs=[vmem] * 4,
        out_shape=[
            weight,
            weight,
            jax.ShapeDtypeStruct((points, 2 * bands, bands), jnp.bfloat16),
            jax.ShapeDtypeStruct((width, PARTS * LANES), jnp.bfloat16),
        ],
        compiler_params=pltpu.CompilerParams(vmem_limit_bytes=48 << 20),
    )(
        levels.reshape(points, bands),
        filled.reshape(points, bands),
        frequencies,
        bose,
        vectors.reshape(points, 2, bands, bands),
        energy_k,
        occupation_k,
    )


def width_kernel(
    block_ref, modes_ref, turned_ref, absorb_ref, count_ref, pick_ref,
    copies_ref, phonon_ref, spread, cycle, moded,
):
    f32 = jnp.float32
    bf16 = jnp.bfloat16
    q_local = modes_ref.shape[0]
    k_local = PARTS // 2
    rows = block_ref.shape[0]
    per_source = 75
    depth = 80
    sources = rows // q_local
    phases = 8
    runs = sources // phases
    block = block_ref[...]
    for part in range(PARTS):
        spread[part] = jnp.dot(
            block, pick_ref[:, part * LANES : (part + 1) * LANES], preferred_element_type=f32
        )
    electron = [None] * k_local
    for q in range(q_local):
        for part in range(2):
            m = modes_ref[q, part].astype(f32)
            cycle[0:MODES, part * LANES : part * LANES + MODES] = m
            cycle[MODES : 2 * MODES, part * LANES : part * LANES + MODES] = m
        sums = [None] * 5
        for phase in range(phases):
            start = (per_source * phase) % MODES
            first = (per_source * phase) // MODES
            left = jnp.concatenate(
                [
                    spread[part, pl.ds(phase * q_local + q, runs, stride=phases * q_local), :]
                    for part in range(PARTS)
                ],
                axis=0,
            )[:, :depth].astype(bf16)
            right = cycle[pl.ds(start, depth), :]
            at = lax.broadcasted_iota(jnp.int32, right.shape, 0)
            until = min(MODES - start, per_source)
            pieces = [(first, jnp.where(at < until, right, 0.0))]
            if until < per_source:
                pieces.append(
                    (first + 1, jnp.where((at >= until) & (at < per_source), right, 0.0))
                )
            for n, piece in pieces:
                value = jnp.dot(left, piece.astype(bf16), preferred_element_type=f32)
                sums[n] = value if sums[n] is None else sums[n] + value
        half = PARTS // 2 * runs
        for n in range(5):
            real = sums[n][:half, :LANES] - sums[n][half:, LANES:]
            imag = sums[n][:half, LANES:] + sums[n][half:, :LANES]
            for k in range(k_local):
                moded[k, 0, pl.ds(n, runs, stride=5), :] = real[k * runs : (k + 1) * runs]
                moded[k, 1, pl.ds(n, runs, stride=5), :] = imag[k * runs : (k + 1) * runs]
        phonon = None
        for k in range(k_local):
            i = q * k_local + k
            right = jnp.concatenate([moded[k, 0], moded[k, 1]], axis=1).astype(bf16)
            both = jnp.dot(turned_ref[i], right, preferred_element_type=f32)
            real = both[:NB, :MODES] + both[NB:, LANES : LANES + MODES]
            imag = both[:NB, LANES : LANES + MODES] - both[NB:, :MODES]
            weight = real * real + imag * imag
            value = jnp.sum(weight * absorb_ref[i], axis=0, keepdims=True)
            electron[k] = value if electron[k] is None else electron[k] + value
            value = jnp.sum(weight * count_ref[i], axis=0, keepdims=True)
            phonon = value if phonon is None else phonon + value
        phonon_ref[q : q + 1, :] = phonon
    copies_ref[...] = jnp.broadcast_to(jnp.concatenate(electron, axis=0)[None], copies_ref.shape)


def widths(block, phonon_modes, turned, absorb, count, pick, members):
    q_local, _, modes, _ = phonon_modes.shape
    rows = block.shape[0]
    vmem = pl.BlockSpec(memory_space=pltpu.VMEM)
    return pl.pallas_call(
        width_kernel,
        in_specs=[vmem] * 6,
        out_specs=[vmem] * 2,
        out_shape=[
            jax.ShapeDtypeStruct((members, PARTS // 2, modes), jnp.float32),
            jax.ShapeDtypeStruct((q_local, modes), jnp.float32),
        ],
        scratch_shapes=[
            pltpu.VMEM((PARTS, rows, LANES), jnp.float32),
            pltpu.VMEM((2 * modes, 2 * LANES), jnp.float32),
            pltpu.VMEM((PARTS // 2, 2, NB, LANES), jnp.float32),
        ],
        compiler_params=pltpu.CompilerParams(vmem_limit_bytes=48 << 20),
    )(block, phonon_modes, turned, absorb, count, pick)


def final_kernel(electron_ref, own_ref, first_ref, second_ref, third_ref, electron_out, phonon_out):
    electron_out[...] = jnp.sum(electron_ref[...], axis=0)
    phonon_out[...] = (own_ref[...] + first_ref[...]) + (second_ref[...] + third_ref[...])


def final_sums(electrons, phonons):
    vmem = pl.BlockSpec(memory_space=pltpu.VMEM)
    return pl.pallas_call(
        final_kernel,
        in_specs=[vmem] * 5,
        out_specs=[vmem] * 2,
        out_shape=[
            jax.ShapeDtypeStruct(electrons.shape[1:], jnp.float32),
            jax.ShapeDtypeStruct(phonons[0].shape, jnp.float32),
        ],
    )(electrons, *phonons)


def chunk_kernel(mine_ref, other_ref, out_ref):
    total = (mine_ref[...].astype(jnp.float32) + other_ref[...].astype(jnp.float32)).astype(
        jnp.bfloat16
    )
    depth = out_ref.shape[1]
    for i in range(out_ref.shape[0]):
        out_ref[i] = total[i * depth : (i + 1) * depth]


def added_chunks(mine, other, depth):
    rows, width = mine.shape
    vmem = pl.BlockSpec(memory_space=pltpu.VMEM)
    return pl.pallas_call(
        chunk_kernel,
        in_specs=[vmem] * 2,
        out_specs=vmem,
        out_shape=jax.ShapeDtypeStruct((rows // depth, depth, width), jnp.bfloat16),
    )(mine, other)


def added(left, right):
    return (left.astype(jnp.float32) + right.astype(jnp.float32)).astype(jnp.bfloat16)


def on_device(
    coupling,
    kpoints,
    qpoints,
    electron_cells,
    phonon_cells,
    phonon_modes,
    band_vectors,
    energies_kq,
    occupations_kq,
    energy_k,
    occupation_k,
    frequencies,
    bose_factors,
):
    q_local = frequencies.shape[0]
    send, keep = products(kpoints, qpoints, electron_cells, phonon_cells, coupling)
    q_total, width = send.shape[1:]
    members = lax.axis_size("ka")
    beside = [(i, i ^ 1) for i in range(members)]
    across = [(i, i ^ 2) for i in range(members)]
    chip = added(keep, lax.ppermute(send, "ka", beside))
    theirs = lax.ppermute(chip[0], "ka", across)
    prepared = tables(
        energies_kq,
        occupations_kq,
        frequencies,
        bose_factors,
        band_vectors,
        energy_k,
        occupation_k,
        width,
    )
    chunks = added_chunks(chip[1], theirs, q_local)
    chunks, prepared, phonon_modes = lax.optimization_barrier((chunks, prepared, phonon_modes))
    arrived = lax.all_to_all(chunks, "pb", 0, 0, tiled=True)
    absorb, count, turned, pick = prepared
    copies, phonon = widths(
        arrived.reshape(q_total, width),
        phonon_modes,
        turned,
        absorb,
        count,
        pick,
        q_total // q_local,
    )
    phonons = [phonon] + [
        lax.ppermute(phonon, "ka", [(i, i ^ flip) for i in range(members)])
        for flip in range(1, members)
    ]
    electrons = lax.all_to_all(copies, "pb", 0, 0, tiled=True)
    return tuple(final_sums(electrons, phonons))


def solution(mesh):
    in_specs = (
        P(None, "ka", "pb", None),
        P(),
        P(),
        P(),
        P(),
        P("pb", None, None, None),
        P("pb", "ka", None, None, None),
        P("pb", "ka", None),
        P("pb", "ka", None),
        P("ka"),
        P("ka"),
        P("pb", None),
        P("pb", None),
    )
    out_specs = (P("ka", None), P("pb", None))
    return jax.shard_map(
        on_device, mesh=mesh, in_specs=in_specs, out_specs=out_specs, check_vma=False
    )
```

```python
import math

import jax
import jax.numpy as jnp
from jax import lax
from jax.experimental import pallas as pl
from jax.experimental.pallas import tpu as pltpu
from jax.sharding import PartitionSpec as P

NB = 40
MODES = 120
NG = 100
SMEARING = 0.05

STRIP = 16
LANES = 128
PARTS = 8


def whole_turn_cosine(ticks):
    rest = ticks - NG * jnp.floor((ticks + 0.5) * (1.0 / NG))
    y = (jnp.abs(rest - NG // 2) - NG // 4) * (2.0 * math.pi / NG)
    z = y * y
    series = -1.0 / 39916800.0
    for term in (1.0 / 362880.0, -1.0 / 5040.0, 1.0 / 120.0, -1.0 / 6.0, 1.0):
        series = series * z + term
    return y * series


def small_dot(left, right, dims):
    return lax.dot_general(left, right, (dims, ((), ())), preferred_element_type=jnp.float32)


def product_kernel(
    kpt_hbm, qpt_hbm, ecell_hbm, pcell_hbm, g_hbm, send_ref, keep_ref,
    kpt_ref, qpt_ref, ecell_ref, pcell_ref, g_ref, table, rows, small_sem, strip_sem,
):
    q_total = qpt_ref.shape[1]
    cells = g_ref.shape[2]
    pairs = g_hbm.shape[1]
    phonons = g_hbm.shape[3]
    groups = kpt_ref.shape[1] // 4
    pitch = table.shape[1] // 2
    f32 = jnp.float32
    bf16 = jnp.bfloat16
    small = [
        pltpu.make_async_copy(source, target, small_sem.at[i])
        for i, (source, target) in enumerate(
            ((kpt_hbm, kpt_ref), (ecell_hbm, ecell_ref), (qpt_hbm, qpt_ref), (pcell_hbm, pcell_ref))
        )
    ]
    for copy in small:
        copy.start()
    strips = []
    for first in range(0, pairs, STRIP):
        part = pl.ds(first, min(STRIP, pairs - first))
        strips.append(
            pltpu.make_async_copy(g_hbm.at[:, part], g_ref.at[:, part], strip_sem.at[len(strips)])
        )
        strips[-1].start()
    blank = jnp.zeros((table.shape[0], pitch - phonons), bf16)
    for part in range(2):
        table[:, part * pitch + phonons : (part + 1) * pitch] = blank
        for slot in range(2):
            for g in range(0, rows.shape[1], table.shape[0]):
                rows[slot, g : g + table.shape[0], part * pitch + phonons : (part + 1) * pitch] = blank
    for copy in small:
        copy.wait()
    mine = lax.axis_index("ka")
    kpt = kpt_ref[...].astype(f32).astype(bf16)
    qpt = qpt_ref[...].astype(f32).astype(bf16)
    ecell = ecell_ref[...].astype(f32).astype(bf16)
    pcell = pcell_ref[...].astype(f32).astype(bf16)
    height = 2 * PARTS * groups
    source = lax.broadcasted_iota(jnp.int32, (kpt.shape[1], height), 0)
    row = lax.broadcasted_iota(jnp.int32, (kpt.shape[1], height), 1)
    wanted = jnp.bitwise_xor((row // PARTS) % groups, mine) * 4 + row % 4
    k_rows = small_dot(kpt, (source == wanted).astype(f32).astype(bf16), ((1,), (0,)))
    source = lax.broadcasted_iota(jnp.int32, (ecell.shape[1], 2 * cells), 0)
    col = lax.broadcasted_iota(jnp.int32, (ecell.shape[1], 2 * cells), 1)
    wanted = mine * cells + jnp.where(col >= cells, col - cells, col)
    e_cols = small_dot(ecell, (source == wanted).astype(f32).astype(bf16), ((1,), (0,)))
    ticks = small_dot(k_rows.astype(bf16), e_cols.astype(bf16), ((0,), (0,)))
    row = lax.broadcasted_iota(jnp.int32, ticks.shape, 0)
    col = lax.broadcasted_iota(jnp.int32, ticks.shape, 1)
    turn = jnp.where(row >= height // 2, 25.0, 0.0)
    turn = turn - jnp.where(row % PARTS >= 4, 25.0, 0.0)
    turn = turn + jnp.where(col >= cells, 25.0, 0.0)
    mix = whole_turn_cosine(ticks + turn).astype(bf16)
    ticks = small_dot(qpt, pcell, ((0,), (0,)))
    table[:, 0:phonons] = whole_turn_cosine(ticks).astype(bf16)
    table[:, pitch : pitch + phonons] = whole_turn_cosine(ticks - 25.0).astype(bf16)

    def mixed_rows(s):
        values = []
        for j in range(STRIP):
            pair = s * STRIP + j
            if pair < pairs:
                both = jnp.concatenate([g_ref[0, pair], g_ref[1, pair]], axis=0)
                values.append(jnp.dot(mix, both, preferred_element_type=f32))
            else:
                values.append(jnp.zeros((height, phonons), f32))
            if j % 2 == 0:
                continue
            for set_ in range(2):
                for g in range(groups):
                    at = (set_ * groups + g) * PARTS
                    two = jnp.concatenate(
                        [values[j - 1][at : at + PARTS], values[j][at : at + PARTS]], axis=0
                    )
                    to = g * LANES + (j - 1) * PARTS
                    rows[s % 2, to : to + 2 * PARTS, set_ * pitch : set_ * pitch + phonons] = (
                        two.astype(bf16)
                    )

    def turned_rows(s):
        turned = small_dot(table[...], rows[s % 2], ((1,), (1,)))
        to = pl.ds(s * LANES, LANES)
        for ref, slot, g in (
            (send_ref, 0, 3), (send_ref, 1, 1), (keep_ref, 0, 2), (keep_ref, 1, 0),
        ):
            ref[slot, :, to] = turned[:, g * LANES : (g + 1) * LANES].astype(bf16)

    for s, strip in enumerate(strips):
        strip.wait()
        mixed_rows(s)
        if s > 0:
            turned_rows(s - 1)
    turned_rows(len(strips) - 1)


def products(kpoints, qpoints, electron_cells, phonon_cells, coupling):
    parts, cells, pairs, phonons = coupling.shape
    k_total = kpoints.shape[1]
    q_total = qpoints.shape[1]
    steps = pl.cdiv(pairs, STRIP)
    pitch = pl.cdiv(phonons, LANES) * LANES
    by_pair = jnp.transpose(coupling, (0, 2, 1, 3))
    out = jax.ShapeDtypeStruct((2, q_total, steps * LANES), jnp.bfloat16)
    points = [
        pltpu.with_memory_space_constraint(a, pltpu.HBM)
        for a in (kpoints, qpoints, electron_cells, phonon_cells)
    ]
    return pl.pallas_call(
        product_kernel,
        in_specs=[pl.BlockSpec(memory_space=pltpu.HBM)] * 5,
        out_specs=[pl.BlockSpec(memory_space=pltpu.VMEM)] * 2,
        out_shape=[out, out],
        scratch_shapes=[pltpu.VMEM(a.shape, a.dtype) for a in points]
        + [
            pltpu.VMEM(by_pair.shape, by_pair.dtype),
            pltpu.VMEM((q_total, 2 * pitch), jnp.bfloat16),
            pltpu.VMEM((2, 2 * k_total * STRIP, 2 * pitch), jnp.bfloat16),
            pltpu.SemaphoreType.DMA((4,)),
            pltpu.SemaphoreType.DMA((steps,)),
        ],
        compiler_params=pltpu.CompilerParams(vmem_limit_bytes=48 << 20),
    )(*points, by_pair)


def table_kernel(
    level_ref, filled_ref, omega_ref, bose_ref, vector_ref, ek_ref, ok_ref,
    absorb_ref, count_ref, turned_ref, pick_ref,
):
    f32 = jnp.float32
    points = level_ref.shape[0]
    q_local = omega_ref.shape[0]
    level = jnp.transpose(level_ref[...])
    filled = jnp.transpose(filled_ref[...])
    scale = 1.0 / (SMEARING * math.sqrt(2.0 * math.pi))
    electron_scale = scale / (256 * NB)
    phonon_scale = scale / (16 * NB)
    for i in range(points):
        q, k = divmod(i, points // q_local)
        offset = ek_ref[k] - level[:, i : i + 1]
        f = filled[:, i : i + 1]
        w = omega_ref[q : q + 1, :]
        n = bose_ref[q : q + 1, :]
        up = jnp.exp(-0.5 * ((offset + w) / SMEARING) ** 2)
        down = jnp.exp(-0.5 * ((offset - w) / SMEARING) ** 2)
        absorb_ref[i] = ((n + f) * up + (n + 1.0 - f) * down) * electron_scale
        count_ref[i] = (ok_ref[k] - f) * up * phonon_scale
        for part in range(2):
            turned_ref[i, part * NB : (part + 1) * NB, :] = jnp.transpose(
                vector_ref[i, part].astype(f32)
            ).astype(jnp.bfloat16)
    lane = lax.broadcasted_iota(jnp.int32, pick_ref.shape, 0)
    col = lax.broadcasted_iota(jnp.int32, pick_ref.shape, 1)
    place = col % LANES
    wanted = (place // STRIP) * LANES + (place % STRIP) * PARTS + col // LANES
    pick_ref[...] = (lane == wanted).astype(f32).astype(jnp.bfloat16)


def tables(levels, filled, frequencies, bose, vectors, energy_k, occupation_k, width):
    q_local, k_local, bands = levels.shape
    points = q_local * k_local
    modes = frequencies.shape[1]
    vmem = pl.BlockSpec(memory_space=pltpu.VMEM)
    smem = pl.BlockSpec(memory_space=pltpu.SMEM)
    weight = jax.ShapeDtypeStruct((points, bands, modes), jnp.float32)
    return pl.pallas_call(
        table_kernel,
        in_specs=[vmem] * 5 + [smem] * 2,
        out_specs=[vmem] * 4,
        out_shape=[
            weight,
            weight,
            jax.ShapeDtypeStruct((points, 2 * bands, bands), jnp.bfloat16),
            jax.ShapeDtypeStruct((width, PARTS * LANES), jnp.bfloat16),
        ],
        compiler_params=pltpu.CompilerParams(vmem_limit_bytes=48 << 20),
    )(
        levels.reshape(points, bands),
        filled.reshape(points, bands),
        frequencies,
        bose,
        vectors.reshape(points, 2, bands, bands),
        energy_k,
        occupation_k,
    )


def width_kernel(
    block_ref, modes_ref, turned_ref, absorb_ref, count_ref, pick_ref,
    copies_ref, phonon_ref, spread, cycle, moded,
):
    f32 = jnp.float32
    bf16 = jnp.bfloat16
    q_local = modes_ref.shape[0]
    k_local = PARTS // 2
    rows = block_ref.shape[0]
    per_source = 75
    depth = 80
    sources = rows // q_local
    phases = 8
    runs = sources // phases
    block = block_ref[...]
    for part in range(PARTS):
        spread[part] = jnp.dot(
            block, pick_ref[:, part * LANES : (part + 1) * LANES], preferred_element_type=f32
        )
    electron = [None] * k_local
    for q in range(q_local):
        for part in range(2):
            m = modes_ref[q, part].astype(f32)
            cycle[0:MODES, part * LANES : part * LANES + MODES] = m
            cycle[MODES : 2 * MODES, part * LANES : part * LANES + MODES] = m
        sums = [None] * 5
        for phase in range(phases):
            start = (per_source * phase) % MODES
            first = (per_source * phase) // MODES
            left = jnp.concatenate(
                [
                    spread[part, pl.ds(phase * q_local + q, runs, stride=phases * q_local), :]
                    for part in range(PARTS)
                ],
                axis=0,
            )[:, :depth].astype(bf16)
            right = cycle[pl.ds(start, depth), :]
            at = lax.broadcasted_iota(jnp.int32, right.shape, 0)
            until = min(MODES - start, per_source)
            pieces = [(first, jnp.where(at < until, right, 0.0))]
            if until < per_source:
                pieces.append(
                    (first + 1, jnp.where((at >= until) & (at < per_source), right, 0.0))
                )
            for n, piece in pieces:
                value = jnp.dot(left, piece.astype(bf16), preferred_element_type=f32)
                sums[n] = value if sums[n] is None else sums[n] + value
        half = PARTS // 2 * runs
        for n in range(5):
            real = sums[n][:half, :LANES] - sums[n][half:, LANES:]
            imag = sums[n][:half, LANES:] + sums[n][half:, :LANES]
            for k in range(k_local):
                moded[k, 0, pl.ds(n, runs, stride=5), :] = real[k * runs : (k + 1) * runs]
                moded[k, 1, pl.ds(n, runs, stride=5), :] = imag[k * runs : (k + 1) * runs]
        phonon = None
        for k in range(k_local):
            i = q * k_local + k
            right = jnp.concatenate([moded[k, 0], moded[k, 1]], axis=1).astype(bf16)
            both = jnp.dot(turned_ref[i], right, preferred_element_type=f32)
            real = both[:NB, :MODES] + both[NB:, LANES : LANES + MODES]
            imag = both[:NB, LANES : LANES + MODES] - both[NB:, :MODES]
            weight = real * real + imag * imag
            value = jnp.sum(weight * absorb_ref[i], axis=0, keepdims=True)
            electron[k] = value if electron[k] is None else electron[k] + value
            value = jnp.sum(weight * count_ref[i], axis=0, keepdims=True)
            phonon = value if phonon is None else phonon + value
        phonon_ref[q : q + 1, :] = phonon
    copies_ref[...] = jnp.broadcast_to(jnp.concatenate(electron, axis=0)[None], copies_ref.shape)


def widths(block, phonon_modes, turned, absorb, count, pick, members):
    q_local, _, modes, _ = phonon_modes.shape
    rows = block.shape[0]
    vmem = pl.BlockSpec(memory_space=pltpu.VMEM)
    return pl.pallas_call(
        width_kernel,
        in_specs=[vmem] * 6,
        out_specs=[vmem] * 2,
        out_shape=[
            jax.ShapeDtypeStruct((members, PARTS // 2, modes), jnp.float32),
            jax.ShapeDtypeStruct((q_local, modes), jnp.float32),
        ],
        scratch_shapes=[
            pltpu.VMEM((PARTS, rows, LANES), jnp.float32),
            pltpu.VMEM((2 * modes, 2 * LANES), jnp.float32),
            pltpu.VMEM((PARTS // 2, 2, NB, LANES), jnp.float32),
        ],
        compiler_params=pltpu.CompilerParams(vmem_limit_bytes=48 << 20),
    )(block, phonon_modes, turned, absorb, count, pick)


def added(left, right):
    return (left.astype(jnp.float32) + right.astype(jnp.float32)).astype(jnp.bfloat16)


def on_device(
    coupling,
    kpoints,
    qpoints,
    electron_cells,
    phonon_cells,
    phonon_modes,
    band_vectors,
    energies_kq,
    occupations_kq,
    energy_k,
    occupation_k,
    frequencies,
    bose_factors,
):
    q_local = frequencies.shape[0]
    send, keep = products(kpoints, qpoints, electron_cells, phonon_cells, coupling)
    q_total, width = send.shape[1:]
    members = lax.axis_size("ka")
    beside = [(i, i ^ 1) for i in range(members)]
    across = [(i, i ^ 2) for i in range(members)]
    chip = added(keep, lax.ppermute(send, "ka", beside))
    theirs = lax.ppermute(chip[0], "ka", across)
    prepared = tables(
        energies_kq,
        occupations_kq,
        frequencies,
        bose_factors,
        band_vectors,
        energy_k,
        occupation_k,
        width,
    )
    chunks = added(chip[1], theirs).reshape(q_total // q_local, q_local, width)
    chunks, prepared, phonon_modes = lax.optimization_barrier((chunks, prepared, phonon_modes))
    arrived = lax.all_to_all(chunks, "pb", 0, 0, tiled=True)
    absorb, count, turned, pick = prepared
    copies, phonon = widths(
        arrived.reshape(q_total, width),
        phonon_modes,
        turned,
        absorb,
        count,
        pick,
        q_total // q_local,
    )
    phonons = [phonon] + [
        lax.ppermute(phonon, "ka", [(i, i ^ flip) for i in range(members)])
        for flip in range(1, members)
    ]
    electrons = lax.all_to_all(copies, "pb", 0, 0, tiled=True)
    return (electrons.sum(axis=0), (phonons[0] + phonons[1]) + (phonons[2] + phonons[3]))


def solution(mesh):
    in_specs = (
        P(None, "ka", "pb", None),
        P(),
        P(),
        P(),
        P(),
        P("pb", None, None, None),
        P("pb", "ka", None, None, None),
        P("pb", "ka", None),
        P("pb", "ka", None),
        P("ka"),
        P("ka"),
        P("pb", None),
        P("pb", None),
    )
    out_specs = (P("ka", None), P("pb", None))
    return jax.shard_map(
        on_device, mesh=mesh, in_specs=in_specs, out_specs=out_specs, check_vma=False
    )
```

```python
import functools
import math

import jax
import jax.numpy as jnp
from jax import lax
from jax.experimental import pallas as pl
from jax.experimental.pallas import tpu as pltpu
from jax.sharding import PartitionSpec as P

NB = 40
MODES = 120
NG = 100
SMEARING = 0.05

STRIP = 16
LANES = 128
PARTS = 8


def whole_turn_cosine(ticks):
    rest = ticks - NG * jnp.floor((ticks + 0.5) * (1.0 / NG))
    y = (jnp.abs(rest - NG // 2) - NG // 4) * (2.0 * math.pi / NG)
    z = y * y
    series = -1.0 / 39916800.0
    for term in (1.0 / 362880.0, -1.0 / 5040.0, 1.0 / 120.0, -1.0 / 6.0, 1.0):
        series = series * z + term
    return y * series


def small_dot(left, right, dims):
    return lax.dot_general(left, right, (dims, ((), ())), preferred_element_type=jnp.float32)


def product_kernel(
    kpt_hbm, qpt_hbm, ecell_hbm, pcell_hbm, g_hbm, send_ref, keep_ref,
    kpt_ref, qpt_ref, ecell_ref, pcell_ref, g_ref, table, rows, small_sem, strip_sem, *, flips,
):
    q_total = qpt_ref.shape[1]
    cells = g_ref.shape[2]
    pairs = g_hbm.shape[1]
    phonons = g_hbm.shape[3]
    groups = len(flips)
    pitch = table.shape[1] // 2
    f32 = jnp.float32
    bf16 = jnp.bfloat16
    small = [
        pltpu.make_async_copy(source, target, small_sem.at[i])
        for i, (source, target) in enumerate(
            ((kpt_hbm, kpt_ref), (ecell_hbm, ecell_ref), (qpt_hbm, qpt_ref), (pcell_hbm, pcell_ref))
        )
    ]
    for copy in small:
        copy.start()
    strips = []
    for first in range(0, pairs, STRIP):
        part = pl.ds(first, min(STRIP, pairs - first))
        strips.append(
            pltpu.make_async_copy(g_hbm.at[:, part], g_ref.at[:, part], strip_sem.at[len(strips)])
        )
        strips[-1].start()
    blank = jnp.zeros((table.shape[0], pitch - phonons), bf16)
    for part in range(2):
        table[:, part * pitch + phonons : (part + 1) * pitch] = blank
        for slot in range(2):
            for g in range(0, rows.shape[1], table.shape[0]):
                rows[slot, g : g + table.shape[0], part * pitch + phonons : (part + 1) * pitch] = blank
    for copy in small:
        copy.wait()
    mine = lax.axis_index("ka")
    kpt = kpt_ref[...].astype(f32).astype(bf16)
    qpt = qpt_ref[...].astype(f32).astype(bf16)
    ecell = ecell_ref[...].astype(f32).astype(bf16)
    pcell = pcell_ref[...].astype(f32).astype(bf16)
    height = 2 * PARTS * groups
    source = lax.broadcasted_iota(jnp.int32, (kpt.shape[1], height), 0)
    row = lax.broadcasted_iota(jnp.int32, (kpt.shape[1], height), 1)
    flip = jnp.where((row // PARTS) % groups == 0, flips[0], flips[1])
    wanted = jnp.bitwise_xor(flip, mine) * 4 + row % 4
    k_rows = small_dot(kpt, (source == wanted).astype(f32).astype(bf16), ((1,), (0,)))
    source = lax.broadcasted_iota(jnp.int32, (ecell.shape[1], 2 * cells), 0)
    col = lax.broadcasted_iota(jnp.int32, (ecell.shape[1], 2 * cells), 1)
    wanted = mine * cells + jnp.where(col >= cells, col - cells, col)
    e_cols = small_dot(ecell, (source == wanted).astype(f32).astype(bf16), ((1,), (0,)))
    ticks = small_dot(k_rows.astype(bf16), e_cols.astype(bf16), ((0,), (0,)))
    row = lax.broadcasted_iota(jnp.int32, ticks.shape, 0)
    col = lax.broadcasted_iota(jnp.int32, ticks.shape, 1)
    turn = jnp.where(row >= height // 2, 25.0, 0.0)
    turn = turn - jnp.where(row % PARTS >= 4, 25.0, 0.0)
    turn = turn + jnp.where(col >= cells, 25.0, 0.0)
    mix = whole_turn_cosine(ticks + turn).astype(bf16)
    ticks = small_dot(qpt, pcell, ((0,), (0,)))
    table[:, 0:phonons] = whole_turn_cosine(ticks).astype(bf16)
    table[:, pitch : pitch + phonons] = whole_turn_cosine(ticks - 25.0).astype(bf16)

    def mixed_rows(s):
        values = []
        for j in range(STRIP):
            pair = s * STRIP + j
            if pair < pairs:
                both = jnp.concatenate([g_ref[0, pair], g_ref[1, pair]], axis=0)
                values.append(jnp.dot(mix, both, preferred_element_type=f32))
            else:
                values.append(jnp.zeros((height, phonons), f32))
            if j % 2 == 0:
                continue
            for set_ in range(2):
                for g in range(groups):
                    at = (set_ * groups + g) * PARTS
                    two = jnp.concatenate(
                        [values[j - 1][at : at + PARTS], values[j][at : at + PARTS]], axis=0
                    )
                    to = g * LANES + (j - 1) * PARTS
                    rows[s % 2, to : to + 2 * PARTS, set_ * pitch : set_ * pitch + phonons] = (
                        two.astype(bf16)
                    )

    def turned_rows(s):
        turned = small_dot(table[...], rows[s % 2], ((1,), (1,)))
        to = pl.ds(s * LANES, LANES)
        send_ref[:, to] = turned[:, :LANES].astype(bf16)
        keep_ref[:, to] = turned[:, LANES:].astype(bf16)

    for s, strip in enumerate(strips):
        strip.wait()
        mixed_rows(s)
        if s > 0:
            turned_rows(s - 1)
    turned_rows(len(strips) - 1)


def products(kpoints, qpoints, electron_cells, phonon_cells, coupling, flips):
    parts, cells, pairs, phonons = coupling.shape
    q_total = qpoints.shape[1]
    steps = pl.cdiv(pairs, STRIP)
    pitch = pl.cdiv(phonons, LANES) * LANES
    by_pair = jnp.transpose(coupling, (0, 2, 1, 3))
    out = jax.ShapeDtypeStruct((q_total, steps * LANES), jnp.bfloat16)
    points = [
        pltpu.with_memory_space_constraint(a, pltpu.HBM)
        for a in (kpoints, qpoints, electron_cells, phonon_cells)
    ]
    return pl.pallas_call(
        functools.partial(product_kernel, flips=flips),
        in_specs=[pl.BlockSpec(memory_space=pltpu.HBM)] * 5,
        out_specs=[pl.BlockSpec(memory_space=pltpu.VMEM)] * 2,
        out_shape=[out, out],
        scratch_shapes=[pltpu.VMEM(a.shape, a.dtype) for a in points]
        + [
            pltpu.VMEM(by_pair.shape, by_pair.dtype),
            pltpu.VMEM((q_total, 2 * pitch), jnp.bfloat16),
            pltpu.VMEM((2, len(flips) * LANES, 2 * pitch), jnp.bfloat16),
            pltpu.SemaphoreType.DMA((4,)),
            pltpu.SemaphoreType.DMA((steps,)),
        ],
        compiler_params=pltpu.CompilerParams(vmem_limit_bytes=48 << 20),
    )(*points, by_pair)


def table_kernel(
    level_ref, filled_ref, omega_ref, bose_ref, vector_ref, ek_ref, ok_ref,
    absorb_ref, count_ref, turned_ref, pick_ref,
):
    f32 = jnp.float32
    points = level_ref.shape[0]
    q_local = omega_ref.shape[0]
    level = jnp.transpose(level_ref[...])
    filled = jnp.transpose(filled_ref[...])
    scale = 1.0 / (SMEARING * math.sqrt(2.0 * math.pi))
    electron_scale = scale / (256 * NB)
    phonon_scale = scale / (16 * NB)
    for i in range(points):
        q, k = divmod(i, points // q_local)
        offset = ek_ref[k] - level[:, i : i + 1]
        f = filled[:, i : i + 1]
        w = omega_ref[q : q + 1, :]
        n = bose_ref[q : q + 1, :]
        up = jnp.exp(-0.5 * ((offset + w) / SMEARING) ** 2)
        down = jnp.exp(-0.5 * ((offset - w) / SMEARING) ** 2)
        absorb_ref[i] = ((n + f) * up + (n + 1.0 - f) * down) * electron_scale
        count_ref[i] = (ok_ref[k] - f) * up * phonon_scale
        for part in range(2):
            turned_ref[i, part * NB : (part + 1) * NB, :] = jnp.transpose(
                vector_ref[i, part].astype(f32)
            ).astype(jnp.bfloat16)
    lane = lax.broadcasted_iota(jnp.int32, pick_ref.shape, 0)
    col = lax.broadcasted_iota(jnp.int32, pick_ref.shape, 1)
    place = col % LANES
    wanted = (place // STRIP) * LANES + (place % STRIP) * PARTS + col // LANES
    pick_ref[...] = (lane == wanted).astype(f32).astype(jnp.bfloat16)


def tables(levels, filled, frequencies, bose, vectors, energy_k, occupation_k, width):
    q_local, k_local, bands = levels.shape
    points = q_local * k_local
    modes = frequencies.shape[1]
    vmem = pl.BlockSpec(memory_space=pltpu.VMEM)
    smem = pl.BlockSpec(memory_space=pltpu.SMEM)
    weight = jax.ShapeDtypeStruct((points, bands, modes), jnp.float32)
    return pl.pallas_call(
        table_kernel,
        in_specs=[vmem] * 5 + [smem] * 2,
        out_specs=[vmem] * 4,
        out_shape=[
            weight,
            weight,
            jax.ShapeDtypeStruct((points, 2 * bands, bands), jnp.bfloat16),
            jax.ShapeDtypeStruct((width, PARTS * LANES), jnp.bfloat16),
        ],
        compiler_params=pltpu.CompilerParams(vmem_limit_bytes=48 << 20),
    )(
        levels.reshape(points, bands),
        filled.reshape(points, bands),
        frequencies,
        bose,
        vectors.reshape(points, 2, bands, bands),
        energy_k,
        occupation_k,
    )


def width_kernel(
    block_ref, modes_ref, turned_ref, absorb_ref, count_ref, pick_ref,
    copies_ref, phonon_ref, spread, cycle, moded,
):
    f32 = jnp.float32
    bf16 = jnp.bfloat16
    q_local = modes_ref.shape[0]
    k_local = PARTS // 2
    rows = block_ref.shape[0]
    per_source = 75
    depth = 80
    sources = rows // q_local
    phases = 8
    runs = sources // phases
    block = block_ref[...]
    for part in range(PARTS):
        spread[part] = jnp.dot(
            block, pick_ref[:, part * LANES : (part + 1) * LANES], preferred_element_type=f32
        )
    electron = [None] * k_local
    for q in range(q_local):
        for part in range(2):
            m = modes_ref[q, part].astype(f32)
            cycle[0:MODES, part * LANES : part * LANES + MODES] = m
            cycle[MODES : 2 * MODES, part * LANES : part * LANES + MODES] = m
        sums = [None] * 5
        for phase in range(phases):
            start = (per_source * phase) % MODES
            first = (per_source * phase) // MODES
            left = jnp.concatenate(
                [
                    spread[part, pl.ds(phase * q_local + q, runs, stride=phases * q_local), :]
                    for part in range(PARTS)
                ],
                axis=0,
            )[:, :depth].astype(bf16)
            right = cycle[pl.ds(start, depth), :]
            at = lax.broadcasted_iota(jnp.int32, right.shape, 0)
            until = min(MODES - start, per_source)
            pieces = [(first, jnp.where(at < until, right, 0.0))]
            if until < per_source:
                pieces.append(
                    (first + 1, jnp.where((at >= until) & (at < per_source), right, 0.0))
                )
            for n, piece in pieces:
                value = jnp.dot(left, piece.astype(bf16), preferred_element_type=f32)
                sums[n] = value if sums[n] is None else sums[n] + value
        half = PARTS // 2 * runs
        for n in range(5):
            real = sums[n][:half, :LANES] - sums[n][half:, LANES:]
            imag = sums[n][:half, LANES:] + sums[n][half:, :LANES]
            for k in range(k_local):
                moded[k, 0, pl.ds(n, runs, stride=5), :] = real[k * runs : (k + 1) * runs]
                moded[k, 1, pl.ds(n, runs, stride=5), :] = imag[k * runs : (k + 1) * runs]
        phonon = None
        for k in range(k_local):
            i = q * k_local + k
            right = jnp.concatenate([moded[k, 0], moded[k, 1]], axis=1).astype(bf16)
            both = jnp.dot(turned_ref[i], right, preferred_element_type=f32)
            real = both[:NB, :MODES] + both[NB:, LANES : LANES + MODES]
            imag = both[:NB, LANES : LANES + MODES] - both[NB:, :MODES]
            weight = real * real + imag * imag
            value = jnp.sum(weight * absorb_ref[i], axis=0, keepdims=True)
            electron[k] = value if electron[k] is None else electron[k] + value
            value = jnp.sum(weight * count_ref[i], axis=0, keepdims=True)
            phonon = value if phonon is None else phonon + value
        phonon_ref[q : q + 1, :] = phonon
    copies_ref[...] = jnp.broadcast_to(jnp.concatenate(electron, axis=0)[None], copies_ref.shape)


def widths(block, phonon_modes, turned, absorb, count, pick, members):
    q_local, _, modes, _ = phonon_modes.shape
    rows = block.shape[0]
    vmem = pl.BlockSpec(memory_space=pltpu.VMEM)
    return pl.pallas_call(
        width_kernel,
        in_specs=[vmem] * 6,
        out_specs=[vmem] * 2,
        out_shape=[
            jax.ShapeDtypeStruct((members, PARTS // 2, modes), jnp.float32),
            jax.ShapeDtypeStruct((q_local, modes), jnp.float32),
        ],
        scratch_shapes=[
            pltpu.VMEM((PARTS, rows, LANES), jnp.float32),
            pltpu.VMEM((2 * modes, 2 * LANES), jnp.float32),
            pltpu.VMEM((PARTS // 2, 2, NB, LANES), jnp.float32),
        ],
        compiler_params=pltpu.CompilerParams(vmem_limit_bytes=48 << 20),
    )(block, phonon_modes, turned, absorb, count, pick)


def added(*arrays):
    return sum(a.astype(jnp.float32) for a in arrays).astype(jnp.bfloat16)


def on_device(
    coupling,
    kpoints,
    qpoints,
    electron_cells,
    phonon_cells,
    phonon_modes,
    band_vectors,
    energies_kq,
    occupations_kq,
    energy_k,
    occupation_k,
    frequencies,
    bose_factors,
):
    q_local = frequencies.shape[0]
    members = lax.axis_size("ka")
    beside = [(i, i ^ 1) for i in range(members)]
    across = [(i, i ^ 2) for i in range(members)]
    send, keep = products(kpoints, qpoints, electron_cells, phonon_cells, coupling, (3, 2))
    q_total, width = send.shape
    chip = added(keep, lax.ppermute(send, "ka", beside))
    chip, kpoints, energy_k = lax.optimization_barrier((chip, kpoints, energy_k))
    theirs = lax.ppermute(chip, "ka", across)
    send, keep = products(kpoints, qpoints, electron_cells, phonon_cells, coupling, (1, 0))
    near = lax.ppermute(send, "ka", beside)
    prepared = tables(
        energies_kq,
        occupations_kq,
        frequencies,
        bose_factors,
        band_vectors,
        energy_k,
        occupation_k,
        width,
    )
    chunks = added(keep, near, theirs).reshape(q_total // q_local, q_local, width)
    chunks, prepared, phonon_modes = lax.optimization_barrier((chunks, prepared, phonon_modes))
    arrived = lax.all_to_all(chunks, "pb", 0, 0, tiled=True)
    absorb, count, turned, pick = prepared
    copies, phonon = widths(
        arrived.reshape(q_total, width),
        phonon_modes,
        turned,
        absorb,
        count,
        pick,
        q_total // q_local,
    )
    phonons = [phonon] + [
        lax.ppermute(phonon, "ka", [(i, i ^ flip) for i in range(members)])
        for flip in range(1, members)
    ]
    electrons = lax.all_to_all(copies, "pb", 0, 0, tiled=True)
    return (electrons.sum(axis=0), (phonons[0] + phonons[1]) + (phonons[2] + phonons[3]))


def solution(mesh):
    in_specs = (
        P(None, "ka", "pb", None),
        P(),
        P(),
        P(),
        P(),
        P("pb", None, None, None),
        P("pb", "ka", None, None, None),
        P("pb", "ka", None),
        P("pb", "ka", None),
        P("ka"),
        P("ka"),
        P("pb", None),
        P("pb", None),
    )
    out_specs = (P("ka", None), P("pb", None))
    return jax.shard_map(
        on_device, mesh=mesh, in_specs=in_specs, out_specs=out_specs, check_vma=False
    )
```

```python
import math

import jax
import jax.numpy as jnp
from jax import lax
from jax.experimental import pallas as pl
from jax.experimental.pallas import tpu as pltpu
from jax.sharding import PartitionSpec as P

NB = 40
MODES = 120
NG = 100
SMEARING = 0.05

STRIP = 16
LANES = 128
PARTS = 8


def whole_turn_cosine(ticks):
    rest = ticks - NG * jnp.floor((ticks + 0.5) * (1.0 / NG))
    y = (jnp.abs(rest - NG // 2) - NG // 4) * (2.0 * math.pi / NG)
    z = y * y
    series = -1.0 / 39916800.0
    for term in (1.0 / 362880.0, -1.0 / 5040.0, 1.0 / 120.0, -1.0 / 6.0, 1.0):
        series = series * z + term
    return y * series


def small_dot(left, right, dims):
    return lax.dot_general(left, right, (dims, ((), ())), preferred_element_type=jnp.float32)


def product_kernel(
    kpt_hbm, qpt_hbm, ecell_hbm, pcell_hbm, g_hbm, near_keep, near_send, far_keep, far_send,
    kpt_ref, qpt_ref, ecell_ref, pcell_ref, g_ref, table, rows, small_sem, strip_sem,
):
    q_total = qpt_ref.shape[1]
    cells = g_ref.shape[2]
    pairs = g_hbm.shape[1]
    phonons = g_hbm.shape[3]
    groups = kpt_ref.shape[1] // 4
    pitch = table.shape[1] // 2
    f32 = jnp.float32
    bf16 = jnp.bfloat16
    small = [
        pltpu.make_async_copy(source, target, small_sem.at[i])
        for i, (source, target) in enumerate(
            ((kpt_hbm, kpt_ref), (ecell_hbm, ecell_ref), (qpt_hbm, qpt_ref), (pcell_hbm, pcell_ref))
        )
    ]
    for copy in small:
        copy.start()
    for copy in small:
        copy.wait()
    strips = []
    for first in range(0, pairs, STRIP):
        part = pl.ds(first, min(STRIP, pairs - first))
        strips.append(
            pltpu.make_async_copy(g_hbm.at[:, part], g_ref.at[:, part], strip_sem.at[len(strips)])
        )
        strips[-1].start()
    blank = jnp.zeros((table.shape[0], pitch - phonons), bf16)
    for part in range(2):
        table[:, part * pitch + phonons : (part + 1) * pitch] = blank
        for slot in range(2):
            for g in range(0, rows.shape[1], table.shape[0]):
                rows[slot, g : g + table.shape[0], part * pitch + phonons : (part + 1) * pitch] = blank
    mine = lax.axis_index("ka")
    kpt = kpt_ref[...].astype(f32).astype(bf16)
    qpt = qpt_ref[...].astype(f32).astype(bf16)
    ecell = ecell_ref[...].astype(f32).astype(bf16)
    pcell = pcell_ref[...].astype(f32).astype(bf16)
    height = 2 * PARTS * groups
    source = lax.broadcasted_iota(jnp.int32, (kpt.shape[1], height), 0)
    row = lax.broadcasted_iota(jnp.int32, (kpt.shape[1], height), 1)
    wanted = jnp.bitwise_xor((row // PARTS) % groups, mine) * 4 + row % 4
    k_rows = small_dot(kpt, (source == wanted).astype(f32).astype(bf16), ((1,), (0,)))
    source = lax.broadcasted_iota(jnp.int32, (ecell.shape[1], 2 * cells), 0)
    col = lax.broadcasted_iota(jnp.int32, (ecell.shape[1], 2 * cells), 1)
    wanted = mine * cells + jnp.where(col >= cells, col - cells, col)
    e_cols = small_dot(ecell, (source == wanted).astype(f32).astype(bf16), ((1,), (0,)))
    ticks = small_dot(k_rows.astype(bf16), e_cols.astype(bf16), ((0,), (0,)))
    row = lax.broadcasted_iota(jnp.int32, ticks.shape, 0)
    col = lax.broadcasted_iota(jnp.int32, ticks.shape, 1)
    turn = jnp.where(row >= height // 2, 25.0, 0.0)
    turn = turn - jnp.where(row % PARTS >= 4, 25.0, 0.0)
    turn = turn + jnp.where(col >= cells, 25.0, 0.0)
    mix = whole_turn_cosine(ticks + turn).astype(bf16)
    ticks = small_dot(qpt, pcell, ((0,), (0,)))
    table[:, 0:phonons] = whole_turn_cosine(ticks).astype(bf16)
    table[:, pitch : pitch + phonons] = whole_turn_cosine(ticks - 25.0).astype(bf16)

    def mixed_rows(s):
        values = []
        for j in range(STRIP):
            pair = s * STRIP + j
            if pair < pairs:
                both = jnp.concatenate([g_ref[0, pair], g_ref[1, pair]], axis=0)
                values.append(jnp.dot(mix, both, preferred_element_type=f32))
            else:
                values.append(jnp.zeros((height, phonons), f32))
            if j % 2 == 0:
                continue
            for set_ in range(2):
                for g in range(groups):
                    at = (set_ * groups + g) * PARTS
                    two = jnp.concatenate(
                        [values[j - 1][at : at + PARTS], values[j][at : at + PARTS]], axis=0
                    )
                    to = g * LANES + (j - 1) * PARTS
                    rows[s % 2, to : to + 2 * PARTS, set_ * pitch : set_ * pitch + phonons] = (
                        two.astype(bf16)
                    )

    def turned_rows(s):
        turned = small_dot(table[...], rows[s % 2], ((1,), (1,)))
        to = pl.ds(s * LANES, LANES)
        for g, ref in enumerate((near_keep, near_send, far_keep, far_send)):
            ref[:, to] = turned[:, g * LANES : (g + 1) * LANES].astype(bf16)

    for s, strip in enumerate(strips):
        strip.wait()
        mixed_rows(s)
        if s > 0:
            turned_rows(s - 1)
    turned_rows(len(strips) - 1)


def products(kpoints, qpoints, electron_cells, phonon_cells, coupling):
    parts, cells, pairs, phonons = coupling.shape
    k_total = kpoints.shape[1]
    q_total = qpoints.shape[1]
    steps = pl.cdiv(pairs, STRIP)
    pitch = pl.cdiv(phonons, LANES) * LANES
    by_pair = jnp.transpose(coupling, (0, 2, 1, 3))
    out = jax.ShapeDtypeStruct((q_total, steps * LANES), jnp.bfloat16)
    points = [
        pltpu.with_memory_space_constraint(a, pltpu.HBM)
        for a in (kpoints, qpoints, electron_cells, phonon_cells)
    ]
    return pl.pallas_call(
        product_kernel,
        in_specs=[pl.BlockSpec(memory_space=pltpu.HBM)] * 5,
        out_specs=[pl.BlockSpec(memory_space=pltpu.VMEM)] * 4,
        out_shape=[out] * 4,
        scratch_shapes=[pltpu.VMEM(a.shape, a.dtype) for a in points]
        + [
            pltpu.VMEM(by_pair.shape, by_pair.dtype),
            pltpu.VMEM((q_total, 2 * pitch), jnp.bfloat16),
            pltpu.VMEM((2, 2 * k_total * STRIP, 2 * pitch), jnp.bfloat16),
            pltpu.SemaphoreType.DMA((4,)),
            pltpu.SemaphoreType.DMA((steps,)),
        ],
        compiler_params=pltpu.CompilerParams(vmem_limit_bytes=48 << 20),
    )(*points, by_pair)


def table_kernel(
    level_ref, filled_ref, omega_ref, bose_ref, vector_ref, ek_ref, ok_ref,
    absorb_ref, count_ref, turned_ref, pick_ref,
):
    f32 = jnp.float32
    points = level_ref.shape[0]
    q_local = omega_ref.shape[0]
    level = jnp.transpose(level_ref[...])
    filled = jnp.transpose(filled_ref[...])
    scale = 1.0 / (SMEARING * math.sqrt(2.0 * math.pi))
    electron_scale = scale / (256 * NB)
    phonon_scale = scale / (16 * NB)
    for i in range(points):
        q, k = divmod(i, points // q_local)
        offset = ek_ref[k] - level[:, i : i + 1]
        f = filled[:, i : i + 1]
        w = omega_ref[q : q + 1, :]
        n = bose_ref[q : q + 1, :]
        up = jnp.exp(-0.5 * ((offset + w) / SMEARING) ** 2)
        down = jnp.exp(-0.5 * ((offset - w) / SMEARING) ** 2)
        absorb_ref[i] = ((n + f) * up + (n + 1.0 - f) * down) * electron_scale
        count_ref[i] = (ok_ref[k] - f) * up * phonon_scale
        for part in range(2):
            turned_ref[i, part * NB : (part + 1) * NB, :] = jnp.transpose(
                vector_ref[i, part].astype(f32)
            ).astype(jnp.bfloat16)
    lane = lax.broadcasted_iota(jnp.int32, pick_ref.shape, 0)
    col = lax.broadcasted_iota(jnp.int32, pick_ref.shape, 1)
    place = col % LANES
    wanted = (place // STRIP) * LANES + (place % STRIP) * PARTS + col // LANES
    pick_ref[...] = (lane == wanted).astype(f32).astype(jnp.bfloat16)


def tables(levels, filled, frequencies, bose, vectors, energy_k, occupation_k, width):
    q_local, k_local, bands = levels.shape
    points = q_local * k_local
    modes = frequencies.shape[1]
    vmem = pl.BlockSpec(memory_space=pltpu.VMEM)
    smem = pl.BlockSpec(memory_space=pltpu.SMEM)
    weight = jax.ShapeDtypeStruct((points, bands, modes), jnp.float32)
    return pl.pallas_call(
        table_kernel,
        in_specs=[vmem] * 5 + [smem] * 2,
        out_specs=[vmem] * 4,
        out_shape=[
            weight,
            weight,
            jax.ShapeDtypeStruct((points, 2 * bands, bands), jnp.bfloat16),
            jax.ShapeDtypeStruct((width, PARTS * LANES), jnp.bfloat16),
        ],
        compiler_params=pltpu.CompilerParams(vmem_limit_bytes=48 << 20),
    )(
        levels.reshape(points, bands),
        filled.reshape(points, bands),
        frequencies,
        bose,
        vectors.reshape(points, 2, bands, bands),
        energy_k,
        occupation_k,
    )


def width_kernel(
    block_ref, modes_ref, turned_ref, absorb_ref, count_ref, pick_ref,
    copies_ref, phonon_ref, spread, cycle, moded,
):
    f32 = jnp.float32
    bf16 = jnp.bfloat16
    q_local = modes_ref.shape[0]
    k_local = PARTS // 2
    rows = block_ref.shape[0]
    per_source = 75
    depth = 80
    sources = rows // q_local
    phases = 8
    runs = sources // phases
    block = block_ref[...]
    for part in range(PARTS):
        spread[part] = jnp.dot(
            block, pick_ref[:, part * LANES : (part + 1) * LANES], preferred_element_type=f32
        )
    electron = [None] * k_local
    for q in range(q_local):
        for part in range(2):
            m = modes_ref[q, part].astype(f32)
            cycle[q, 0:MODES, part * LANES : part * LANES + MODES] = m
            cycle[q, MODES : 2 * MODES, part * LANES : part * LANES + MODES] = m
        sums = [None] * 5
        for phase in range(phases):
            start = (per_source * phase) % MODES
            first = (per_source * phase) // MODES
            left = jnp.concatenate(
                [
                    spread[part, pl.ds(phase * q_local + q, runs, stride=phases * q_local), :]
                    for part in range(PARTS)
                ],
                axis=0,
            )[:, :depth].astype(bf16)
            right = cycle[q, pl.ds(start, depth), :]
            at = lax.broadcasted_iota(jnp.int32, right.shape, 0)
            until = min(MODES - start, per_source)
            pieces = [(first, jnp.where(at < until, right, 0.0))]
            if until < per_source:
                pieces.append(
                    (first + 1, jnp.where((at >= until) & (at < per_source), right, 0.0))
                )
            for n, piece in pieces:
                value = jnp.dot(left, piece.astype(bf16), preferred_element_type=f32)
                sums[n] = value if sums[n] is None else sums[n] + value
        half = PARTS // 2 * runs
        for n in range(5):
            real = sums[n][:half, :LANES] - sums[n][half:, LANES:]
            imag = sums[n][:half, LANES:] + sums[n][half:, :LANES]
            for k in range(k_local):
                moded[q * k_local + k, 0, pl.ds(n, runs, stride=5), :] = real[k * runs : (k + 1) * runs]
                moded[q * k_local + k, 1, pl.ds(n, runs, stride=5), :] = imag[k * runs : (k + 1) * runs]
        phonon = None
        for k in range(k_local):
            i = q * k_local + k
            right = jnp.concatenate([moded[i, 0], moded[i, 1]], axis=1).astype(bf16)
            both = jnp.dot(turned_ref[i], right, preferred_element_type=f32)
            real = both[:NB, :MODES] + both[NB:, LANES : LANES + MODES]
            imag = both[:NB, LANES : LANES + MODES] - both[NB:, :MODES]
            weight = real * real + imag * imag
            value = jnp.sum(weight * absorb_ref[i], axis=0, keepdims=True)
            electron[k] = value if electron[k] is None else electron[k] + value
            value = jnp.sum(weight * count_ref[i], axis=0, keepdims=True)
            phonon = value if phonon is None else phonon + value
        phonon_ref[q : q + 1, :] = phonon
    copies_ref[...] = jnp.broadcast_to(jnp.concatenate(electron, axis=0)[None], copies_ref.shape)


def widths(block, phonon_modes, turned, absorb, count, pick, members):
    q_local, _, modes, _ = phonon_modes.shape
    rows = block.shape[0]
    vmem = pl.BlockSpec(memory_space=pltpu.VMEM)
    return pl.pallas_call(
        width_kernel,
        in_specs=[vmem] * 6,
        out_specs=[vmem] * 2,
        out_shape=[
            jax.ShapeDtypeStruct((members, PARTS // 2, modes), jnp.float32),
            jax.ShapeDtypeStruct((q_local, modes), jnp.float32),
        ],
        scratch_shapes=[
            pltpu.VMEM((PARTS, rows, LANES), jnp.float32),
            pltpu.VMEM((q_local, 2 * modes, 2 * LANES), jnp.float32),
            pltpu.VMEM((q_local * PARTS // 2, 2, NB, LANES), jnp.float32),
        ],
        compiler_params=pltpu.CompilerParams(vmem_limit_bytes=48 << 20),
    )(block, phonon_modes, turned, absorb, count, pick)


def added(*arrays):
    return sum(a.astype(jnp.float32) for a in arrays).astype(jnp.bfloat16)


def on_device(
    coupling,
    kpoints,
    qpoints,
    electron_cells,
    phonon_cells,
    phonon_modes,
    band_vectors,
    energies_kq,
    occupations_kq,
    energy_k,
    occupation_k,
    frequencies,
    bose_factors,
):
    q_local = frequencies.shape[0]
    members = lax.axis_size("ka")
    beside = [(i, i ^ 1) for i in range(members)]
    across = [(i, i ^ 2) for i in range(members)]
    near_keep, near_send, far_keep, far_send = products(
        kpoints, qpoints, electron_cells, phonon_cells, coupling
    )
    q_total, width = far_send.shape
    chip = added(far_keep, lax.ppermute(far_send, "ka", beside))
    chip, near_send, energy_k = lax.optimization_barrier((chip, near_send, energy_k))
    theirs = lax.ppermute(chip, "ka", across)
    near = lax.ppermute(near_send, "ka", beside)
    prepared = tables(
        energies_kq,
        occupations_kq,
        frequencies,
        bose_factors,
        band_vectors,
        energy_k,
        occupation_k,
        width,
    )
    chunks = added(near_keep, near, theirs).reshape(q_total // q_local, q_local, width)
    chunks, prepared, phonon_modes = lax.optimization_barrier((chunks, prepared, phonon_modes))
    arrived = lax.all_to_all(chunks, "pb", 0, 0, tiled=True)
    absorb, count, turned, pick = prepared
    copies, phonon = widths(
        arrived.reshape(q_total, width),
        phonon_modes,
        turned,
        absorb,
        count,
        pick,
        q_total // q_local,
    )
    phonons = [phonon] + [
        lax.ppermute(phonon, "ka", [(i, i ^ flip) for i in range(members)])
        for flip in range(1, members)
    ]
    electrons = lax.all_to_all(copies, "pb", 0, 0, tiled=True)
    return (electrons.sum(axis=0), (phonons[0] + phonons[1]) + (phonons[2] + phonons[3]))


def solution(mesh):
    in_specs = (
        P(None, "ka", "pb", None),
        P(),
        P(),
        P(),
        P(),
        P("pb", None, None, None),
        P("pb", "ka", None, None, None),
        P("pb", "ka", None),
        P("pb", "ka", None),
        P("ka"),
        P("ka"),
        P("pb", None),
        P("pb", None),
    )
    out_specs = (P("ka", None), P("pb", None))
    return jax.shard_map(
        on_device, mesh=mesh, in_specs=in_specs, out_specs=out_specs, check_vma=False
    )
```

```python
import functools
import math

import jax
import jax.numpy as jnp
from jax import lax
from jax.experimental import pallas as pl
from jax.experimental.pallas import tpu as pltpu
from jax.sharding import PartitionSpec as P

NB = 40
MODES = 120
NG = 100
SMEARING = 0.05

STRIP = 16
LANES = 128
PARTS = 8
AHEAD = 3


def whole_turn_cosine(ticks):
    rest = ticks - NG * jnp.floor((ticks + 0.5) * (1.0 / NG))
    y = (jnp.abs(rest - NG // 2) - NG // 4) * (2.0 * math.pi / NG)
    z = y * y
    series = -1.0 / 39916800.0
    for term in (1.0 / 362880.0, -1.0 / 5040.0, 1.0 / 120.0, -1.0 / 6.0, 1.0):
        series = series * z + term
    return y * series


def small_dot(left, right, dims):
    return lax.dot_general(left, right, (dims, ((), ())), preferred_element_type=jnp.float32)


def product_kernel(
    kpt_hbm, qpt_hbm, ecell_hbm, pcell_hbm, g_hbm, near_keep, near_send, far_keep, far_send,
    kpt_ref, qpt_ref, ecell_ref, pcell_ref, g_ref, table, rows, small_sem, strip_sem, *, first_pair,
):
    q_total = qpt_ref.shape[1]
    cells = g_ref.shape[2]
    pairs = g_ref.shape[1]
    phonons = g_ref.shape[3]
    groups = kpt_ref.shape[1] // 4
    pitch = table.shape[1] // 2
    f32 = jnp.float32
    bf16 = jnp.bfloat16
    small = [
        pltpu.make_async_copy(source, target, small_sem.at[i])
        for i, (source, target) in enumerate(
            ((kpt_hbm, kpt_ref), (ecell_hbm, ecell_ref), (qpt_hbm, qpt_ref), (pcell_hbm, pcell_ref))
        )
    ]
    for copy in small:
        copy.start()
    for copy in small:
        copy.wait()
    strips = []
    for first in range(0, pairs, STRIP):
        size = min(STRIP, pairs - first)
        strips.append(
            pltpu.make_async_copy(
                g_hbm.at[:, pl.ds(first_pair + first, size)],
                g_ref.at[:, pl.ds(first, size)],
                strip_sem.at[len(strips)],
            )
        )
        strips[-1].start()
    blank = jnp.zeros((table.shape[0], pitch - phonons), bf16)
    for part in range(2):
        table[:, part * pitch + phonons : (part + 1) * pitch] = blank
        for slot in range(2):
            for g in range(0, rows.shape[1], table.shape[0]):
                rows[slot, g : g + table.shape[0], part * pitch + phonons : (part + 1) * pitch] = blank
    mine = lax.axis_index("ka")
    kpt = kpt_ref[...].astype(f32).astype(bf16)
    qpt = qpt_ref[...].astype(f32).astype(bf16)
    ecell = ecell_ref[...].astype(f32).astype(bf16)
    pcell = pcell_ref[...].astype(f32).astype(bf16)
    height = 2 * PARTS * groups
    source = lax.broadcasted_iota(jnp.int32, (kpt.shape[1], height), 0)
    row = lax.broadcasted_iota(jnp.int32, (kpt.shape[1], height), 1)
    wanted = jnp.bitwise_xor((row // PARTS) % groups, mine) * 4 + row % 4
    k_rows = small_dot(kpt, (source == wanted).astype(f32).astype(bf16), ((1,), (0,)))
    source = lax.broadcasted_iota(jnp.int32, (ecell.shape[1], 2 * cells), 0)
    col = lax.broadcasted_iota(jnp.int32, (ecell.shape[1], 2 * cells), 1)
    wanted = mine * cells + jnp.where(col >= cells, col - cells, col)
    e_cols = small_dot(ecell, (source == wanted).astype(f32).astype(bf16), ((1,), (0,)))
    ticks = small_dot(k_rows.astype(bf16), e_cols.astype(bf16), ((0,), (0,)))
    row = lax.broadcasted_iota(jnp.int32, ticks.shape, 0)
    col = lax.broadcasted_iota(jnp.int32, ticks.shape, 1)
    turn = jnp.where(row >= height // 2, 25.0, 0.0)
    turn = turn - jnp.where(row % PARTS >= 4, 25.0, 0.0)
    turn = turn + jnp.where(col >= cells, 25.0, 0.0)
    mix = whole_turn_cosine(ticks + turn).astype(bf16)
    ticks = small_dot(qpt, pcell, ((0,), (0,)))
    table[:, 0:phonons] = whole_turn_cosine(ticks).astype(bf16)
    table[:, pitch : pitch + phonons] = whole_turn_cosine(ticks - 25.0).astype(bf16)

    def mixed_rows(s):
        values = []
        for j in range(STRIP):
            pair = s * STRIP + j
            if pair < pairs:
                both = jnp.concatenate([g_ref[0, pair], g_ref[1, pair]], axis=0)
                values.append(jnp.dot(mix, both, preferred_element_type=f32))
            else:
                values.append(jnp.zeros((height, phonons), f32))
            if j % 2 == 0:
                continue
            for set_ in range(2):
                for g in range(groups):
                    at = (set_ * groups + g) * PARTS
                    two = jnp.concatenate(
                        [values[j - 1][at : at + PARTS], values[j][at : at + PARTS]], axis=0
                    )
                    to = g * LANES + (j - 1) * PARTS
                    rows[s % 2, to : to + 2 * PARTS, set_ * pitch : set_ * pitch + phonons] = (
                        two.astype(bf16)
                    )

    def turned_rows(s):
        turned = small_dot(table[...], rows[s % 2], ((1,), (1,)))
        to = pl.ds(s * LANES, LANES)
        for g, ref in enumerate((near_keep, near_send, far_keep, far_send)):
            ref[:, to] = turned[:, g * LANES : (g + 1) * LANES].astype(bf16)

    for s, strip in enumerate(strips):
        strip.wait()
        mixed_rows(s)
        if s > 0:
            turned_rows(s - 1)
    turned_rows(len(strips) - 1)


def products(kpoints, qpoints, electron_cells, phonon_cells, coupling, first_pair, pairs):
    parts, cells, _, phonons = coupling.shape
    k_total = kpoints.shape[1]
    q_total = qpoints.shape[1]
    steps = pl.cdiv(pairs, STRIP)
    pitch = pl.cdiv(phonons, LANES) * LANES
    by_pair = jnp.transpose(coupling, (0, 2, 1, 3))
    out = jax.ShapeDtypeStruct((q_total, steps * LANES), jnp.bfloat16)
    points = [
        pltpu.with_memory_space_constraint(a, pltpu.HBM)
        for a in (kpoints, qpoints, electron_cells, phonon_cells)
    ]
    return pl.pallas_call(
        functools.partial(product_kernel, first_pair=first_pair),
        in_specs=[pl.BlockSpec(memory_space=pltpu.HBM)] * 5,
        out_specs=[pl.BlockSpec(memory_space=pltpu.VMEM)] * 4,
        out_shape=[out] * 4,
        scratch_shapes=[pltpu.VMEM(a.shape, a.dtype) for a in points]
        + [
            pltpu.VMEM((parts, pairs, cells, phonons), by_pair.dtype),
            pltpu.VMEM((q_total, 2 * pitch), jnp.bfloat16),
            pltpu.VMEM((2, 2 * k_total * STRIP, 2 * pitch), jnp.bfloat16),
            pltpu.SemaphoreType.DMA((4,)),
            pltpu.SemaphoreType.DMA((steps,)),
        ],
        compiler_params=pltpu.CompilerParams(vmem_limit_bytes=48 << 20),
    )(*points, by_pair)


def table_kernel(
    level_ref, filled_ref, omega_ref, bose_ref, vector_ref, ek_ref, ok_ref,
    absorb_ref, count_ref, turned_ref, pick_ref,
):
    f32 = jnp.float32
    points = level_ref.shape[0]
    q_local = omega_ref.shape[0]
    level = jnp.transpose(level_ref[...])
    filled = jnp.transpose(filled_ref[...])
    scale = 1.0 / (SMEARING * math.sqrt(2.0 * math.pi))
    electron_scale = scale / (256 * NB)
    phonon_scale = scale / (16 * NB)
    for i in range(points):
        q, k = divmod(i, points // q_local)
        offset = ek_ref[k] - level[:, i : i + 1]
        f = filled[:, i : i + 1]
        w = omega_ref[q : q + 1, :]
        n = bose_ref[q : q + 1, :]
        up = jnp.exp(-0.5 * ((offset + w) / SMEARING) ** 2)
        down = jnp.exp(-0.5 * ((offset - w) / SMEARING) ** 2)
        absorb_ref[i] = ((n + f) * up + (n + 1.0 - f) * down) * electron_scale
        count_ref[i] = (ok_ref[k] - f) * up * phonon_scale
        for part in range(2):
            turned_ref[i, part * NB : (part + 1) * NB, :] = jnp.transpose(
                vector_ref[i, part].astype(f32)
            ).astype(jnp.bfloat16)
    lane = lax.broadcasted_iota(jnp.int32, pick_ref.shape, 0)
    col = lax.broadcasted_iota(jnp.int32, pick_ref.shape, 1)
    place = col % LANES
    wanted = (place // STRIP) * LANES + (place % STRIP) * PARTS + col // LANES
    pick_ref[...] = (lane == wanted).astype(f32).astype(jnp.bfloat16)


def tables(levels, filled, frequencies, bose, vectors, energy_k, occupation_k, width):
    q_local, k_local, bands = levels.shape
    points = q_local * k_local
    modes = frequencies.shape[1]
    vmem = pl.BlockSpec(memory_space=pltpu.VMEM)
    smem = pl.BlockSpec(memory_space=pltpu.SMEM)
    weight = jax.ShapeDtypeStruct((points, bands, modes), jnp.float32)
    return pl.pallas_call(
        table_kernel,
        in_specs=[vmem] * 5 + [smem] * 2,
        out_specs=[vmem] * 4,
        out_shape=[
            weight,
            weight,
            jax.ShapeDtypeStruct((points, 2 * bands, bands), jnp.bfloat16),
            jax.ShapeDtypeStruct((width, PARTS * LANES), jnp.bfloat16),
        ],
        compiler_params=pltpu.CompilerParams(vmem_limit_bytes=48 << 20),
    )(
        levels.reshape(points, bands),
        filled.reshape(points, bands),
        frequencies,
        bose,
        vectors.reshape(points, 2, bands, bands),
        energy_k,
        occupation_k,
    )


def width_kernel(
    block_ref, modes_ref, turned_ref, absorb_ref, count_ref, pick_ref,
    copies_ref, phonon_ref, spread, cycle, moded,
):
    f32 = jnp.float32
    bf16 = jnp.bfloat16
    q_local = modes_ref.shape[0]
    k_local = PARTS // 2
    rows = block_ref.shape[0]
    per_source = 75
    depth = 80
    sources = rows // q_local
    phases = 8
    runs = sources // phases
    block = block_ref[...]
    for part in range(PARTS):
        spread[part] = jnp.dot(
            block, pick_ref[:, part * LANES : (part + 1) * LANES], preferred_element_type=f32
        )
    electron = [None] * k_local
    for q in range(q_local):
        for part in range(2):
            m = modes_ref[q, part].astype(f32)
            cycle[q, 0:MODES, part * LANES : part * LANES + MODES] = m
            cycle[q, MODES : 2 * MODES, part * LANES : part * LANES + MODES] = m
        sums = [None] * 5
        for phase in range(phases):
            start = (per_source * phase) % MODES
            first = (per_source * phase) // MODES
            left = jnp.concatenate(
                [
                    spread[part, pl.ds(phase * q_local + q, runs, stride=phases * q_local), :]
                    for part in range(PARTS)
                ],
                axis=0,
            )[:, :depth].astype(bf16)
            right = cycle[q, pl.ds(start, depth), :]
            at = lax.broadcasted_iota(jnp.int32, right.shape, 0)
            until = min(MODES - start, per_source)
            pieces = [(first, jnp.where(at < until, right, 0.0))]
            if until < per_source:
                pieces.append(
                    (first + 1, jnp.where((at >= until) & (at < per_source), right, 0.0))
                )
            for n, piece in pieces:
                value = jnp.dot(left, piece.astype(bf16), preferred_element_type=f32)
                sums[n] = value if sums[n] is None else sums[n] + value
        half = PARTS // 2 * runs
        for n in range(5):
            real = sums[n][:half, :LANES] - sums[n][half:, LANES:]
            imag = sums[n][:half, LANES:] + sums[n][half:, :LANES]
            for k in range(k_local):
                moded[q * k_local + k, 0, pl.ds(n, runs, stride=5), :] = real[k * runs : (k + 1) * runs]
                moded[q * k_local + k, 1, pl.ds(n, runs, stride=5), :] = imag[k * runs : (k + 1) * runs]
        phonon = None
        for k in range(k_local):
            i = q * k_local + k
            right = jnp.concatenate([moded[i, 0], moded[i, 1]], axis=1).astype(bf16)
            both = jnp.dot(turned_ref[i], right, preferred_element_type=f32)
            real = both[:NB, :MODES] + both[NB:, LANES : LANES + MODES]
            imag = both[:NB, LANES : LANES + MODES] - both[NB:, :MODES]
            weight = real * real + imag * imag
            value = jnp.sum(weight * absorb_ref[i], axis=0, keepdims=True)
            electron[k] = value if electron[k] is None else electron[k] + value
            value = jnp.sum(weight * count_ref[i], axis=0, keepdims=True)
            phonon = value if phonon is None else phonon + value
        phonon_ref[q : q + 1, :] = phonon
    copies_ref[...] = jnp.broadcast_to(jnp.concatenate(electron, axis=0)[None], copies_ref.shape)


def widths(block, phonon_modes, turned, absorb, count, pick, members):
    q_local, _, modes, _ = phonon_modes.shape
    rows = block.shape[0]
    vmem = pl.BlockSpec(memory_space=pltpu.VMEM)
    return pl.pallas_call(
        width_kernel,
        in_specs=[vmem] * 6,
        out_specs=[vmem] * 2,
        out_shape=[
            jax.ShapeDtypeStruct((members, PARTS // 2, modes), jnp.float32),
            jax.ShapeDtypeStruct((q_local, modes), jnp.float32),
        ],
        scratch_shapes=[
            pltpu.VMEM((PARTS, rows, LANES), jnp.float32),
            pltpu.VMEM((q_local, 2 * modes, 2 * LANES), jnp.float32),
            pltpu.VMEM((q_local * PARTS // 2, 2, NB, LANES), jnp.float32),
        ],
        compiler_params=pltpu.CompilerParams(vmem_limit_bytes=48 << 20),
    )(block, phonon_modes, turned, absorb, count, pick)


def added(*arrays):
    return sum(a.astype(jnp.float32) for a in arrays).astype(jnp.bfloat16)


def on_device(
    coupling,
    kpoints,
    qpoints,
    electron_cells,
    phonon_cells,
    phonon_modes,
    band_vectors,
    energies_kq,
    occupations_kq,
    energy_k,
    occupation_k,
    frequencies,
    bose_factors,
):
    q_local = frequencies.shape[0]
    members = lax.axis_size("ka")
    beside = [(i, i ^ 1) for i in range(members)]
    across = [(i, i ^ 2) for i in range(members)]
    pairs = coupling.shape[2]
    ahead = min(AHEAD * STRIP, pairs)
    near_parts = []
    far_parts = []
    for first, count in ((0, ahead), (ahead, pairs - ahead)):
        near_keep, near_send, far_keep, far_send = products(
            kpoints, qpoints, electron_cells, phonon_cells, coupling, first, count
        )
        chip = added(far_keep, lax.ppermute(far_send, "ka", beside))
        near_parts.append((near_keep, near_send))
        chip, kpoints, energy_k, near_parts = lax.optimization_barrier(
            (chip, kpoints, energy_k, near_parts)
        )
        far_parts.append(lax.ppermute(chip, "ka", across))
    q_total = qpoints.shape[1]
    sums = [
        added(near_keep, lax.ppermute(near_send, "ka", beside), theirs)
        for (near_keep, near_send), theirs in zip(near_parts, far_parts)
    ]
    whole = jnp.concatenate(sums, axis=1)
    width = whole.shape[1]
    prepared = tables(
        energies_kq,
        occupations_kq,
        frequencies,
        bose_factors,
        band_vectors,
        energy_k,
        occupation_k,
        width,
    )
    chunks = whole.reshape(q_total // q_local, q_local, width)
    chunks, prepared, phonon_modes = lax.optimization_barrier((chunks, prepared, phonon_modes))
    arrived = lax.all_to_all(chunks, "pb", 0, 0, tiled=True)
    absorb, count, turned, pick = prepared
    copies, phonon = widths(
        arrived.reshape(q_total, width),
        phonon_modes,
        turned,
        absorb,
        count,
        pick,
        q_total // q_local,
    )
    phonons = [phonon] + [
        lax.ppermute(phonon, "ka", [(i, i ^ flip) for i in range(members)])
        for flip in range(1, members)
    ]
    electrons = lax.all_to_all(copies, "pb", 0, 0, tiled=True)
    return (electrons.sum(axis=0), (phonons[0] + phonons[1]) + (phonons[2] + phonons[3]))


def solution(mesh):
    in_specs = (
        P(None, "ka", "pb", None),
        P(),
        P(),
        P(),
        P(),
        P("pb", None, None, None),
        P("pb", "ka", None, None, None),
        P("pb", "ka", None),
        P("pb", "ka", None),
        P("ka"),
        P("ka"),
        P("pb", None),
        P("pb", None),
    )
    out_specs = (P("ka", None), P("pb", None))
    return jax.shard_map(
        on_device, mesh=mesh, in_specs=in_specs, out_specs=out_specs, check_vma=False
    )
```

```python
import math

import jax
import jax.numpy as jnp
from jax import lax
from jax.experimental import pallas as pl
from jax.experimental.pallas import tpu as pltpu
from jax.sharding import PartitionSpec as P

NB = 40
MODES = 120
NG = 100
SMEARING = 0.05

STRIP = 16
LANES = 128
PARTS = 8


def whole_turn_cosine(ticks):
    rest = ticks - NG * jnp.floor((ticks + 0.5) * (1.0 / NG))
    y = (jnp.abs(rest - NG // 2) - NG // 4) * (2.0 * math.pi / NG)
    z = y * y
    series = -1.0 / 39916800.0
    for term in (1.0 / 362880.0, -1.0 / 5040.0, 1.0 / 120.0, -1.0 / 6.0, 1.0):
        series = series * z + term
    return y * series


def small_dot(left, right, dims):
    return lax.dot_general(left, right, (dims, ((), ())), preferred_element_type=jnp.float32)


def product_kernel(
    kpt_hbm, qpt_hbm, ecell_hbm, pcell_hbm, g_hbm, near_keep, near_send, far_keep, far_send,
    kpt_ref, qpt_ref, ecell_ref, pcell_ref, g_ref, table, rows, small_sem, strip_sem,
):
    q_total = qpt_ref.shape[1]
    cells = g_ref.shape[2]
    pairs = g_hbm.shape[1]
    phonons = g_hbm.shape[3]
    groups = kpt_ref.shape[1] // 4
    pitch = table.shape[1] // 2
    f32 = jnp.float32
    bf16 = jnp.bfloat16
    small = [
        pltpu.make_async_copy(source, target, small_sem.at[i])
        for i, (source, target) in enumerate(
            ((kpt_hbm, kpt_ref), (ecell_hbm, ecell_ref), (qpt_hbm, qpt_ref), (pcell_hbm, pcell_ref))
        )
    ]
    for copy in small:
        copy.start()
    for copy in small:
        copy.wait()
    strips = []
    for first in range(0, pairs, STRIP):
        part = pl.ds(first, min(STRIP, pairs - first))
        strips.append(
            pltpu.make_async_copy(g_hbm.at[:, part], g_ref.at[:, part], strip_sem.at[len(strips)])
        )
        strips[-1].start()
    blank = jnp.zeros((table.shape[0], pitch - phonons), bf16)
    for part in range(2):
        table[:, part * pitch + phonons : (part + 1) * pitch] = blank
        for slot in range(2):
            for g in range(0, rows.shape[1], table.shape[0]):
                rows[slot, g : g + table.shape[0], part * pitch + phonons : (part + 1) * pitch] = blank
    mine = lax.axis_index("ka")
    kpt = kpt_ref[...].astype(f32).astype(bf16)
    qpt = qpt_ref[...].astype(f32).astype(bf16)
    ecell = ecell_ref[...].astype(f32).astype(bf16)
    pcell = pcell_ref[...].astype(f32).astype(bf16)
    height = 2 * PARTS * groups
    source = lax.broadcasted_iota(jnp.int32, (kpt.shape[1], height), 0)
    row = lax.broadcasted_iota(jnp.int32, (kpt.shape[1], height), 1)
    wanted = jnp.bitwise_xor((row // PARTS) % groups, mine) * 4 + row % 4
    k_rows = small_dot(kpt, (source == wanted).astype(f32).astype(bf16), ((1,), (0,)))
    source = lax.broadcasted_iota(jnp.int32, (ecell.shape[1], 2 * cells), 0)
    col = lax.broadcasted_iota(jnp.int32, (ecell.shape[1], 2 * cells), 1)
    wanted = mine * cells + jnp.where(col >= cells, col - cells, col)
    e_cols = small_dot(ecell, (source == wanted).astype(f32).astype(bf16), ((1,), (0,)))
    ticks = small_dot(k_rows.astype(bf16), e_cols.astype(bf16), ((0,), (0,)))
    row = lax.broadcasted_iota(jnp.int32, ticks.shape, 0)
    col = lax.broadcasted_iota(jnp.int32, ticks.shape, 1)
    turn = jnp.where(row >= height // 2, 25.0, 0.0)
    turn = turn - jnp.where(row % PARTS >= 4, 25.0, 0.0)
    turn = turn + jnp.where(col >= cells, 25.0, 0.0)
    mix = whole_turn_cosine(ticks + turn).astype(bf16)
    ticks = small_dot(qpt, pcell, ((0,), (0,)))
    table[:, 0:phonons] = whole_turn_cosine(ticks).astype(bf16)
    table[:, pitch : pitch + phonons] = whole_turn_cosine(ticks - 25.0).astype(bf16)

    def mixed_rows(s):
        values = []
        for j in range(STRIP):
            pair = s * STRIP + j
            if pair < pairs:
                both = jnp.concatenate([g_ref[0, pair], g_ref[1, pair]], axis=0)
                values.append(jnp.dot(mix, both, preferred_element_type=f32))
            else:
                values.append(jnp.zeros((height, phonons), f32))
            if j % 2 == 0:
                continue
            for set_ in range(2):
                for g in range(groups):
                    at = (set_ * groups + g) * PARTS
                    two = jnp.concatenate(
                        [values[j - 1][at : at + PARTS], values[j][at : at + PARTS]], axis=0
                    )
                    to = g * LANES + (j - 1) * PARTS
                    rows[s % 2, to : to + 2 * PARTS, set_ * pitch : set_ * pitch + phonons] = (
                        two.astype(bf16)
                    )

    def turned_rows(s):
        turned = small_dot(table[...], rows[s % 2], ((1,), (1,)))
        to = pl.ds(s * LANES, LANES)
        for g, ref in enumerate((near_keep, near_send, far_keep, far_send)):
            ref[:, to] = turned[:, g * LANES : (g + 1) * LANES].astype(bf16)

    for s, strip in enumerate(strips):
        strip.wait()
        mixed_rows(s)
        if s > 0:
            turned_rows(s - 1)
    turned_rows(len(strips) - 1)


def products(kpoints, qpoints, electron_cells, phonon_cells, coupling):
    parts, cells, pairs, phonons = coupling.shape
    k_total = kpoints.shape[1]
    q_total = qpoints.shape[1]
    steps = pl.cdiv(pairs, STRIP)
    pitch = pl.cdiv(phonons, LANES) * LANES
    by_pair = jnp.transpose(coupling, (0, 2, 1, 3))
    out = jax.ShapeDtypeStruct((q_total, steps * LANES), jnp.bfloat16)
    points = [
        pltpu.with_memory_space_constraint(a, pltpu.HBM)
        for a in (kpoints, qpoints, electron_cells, phonon_cells)
    ]
    return pl.pallas_call(
        product_kernel,
        in_specs=[pl.BlockSpec(memory_space=pltpu.HBM)] * 5,
        out_specs=[pl.BlockSpec(memory_space=pltpu.VMEM)] * 4,
        out_shape=[out] * 4,
        scratch_shapes=[pltpu.VMEM(a.shape, a.dtype) for a in points]
        + [
            pltpu.VMEM(by_pair.shape, by_pair.dtype),
            pltpu.VMEM((q_total, 2 * pitch), jnp.bfloat16),
            pltpu.VMEM((2, 2 * k_total * STRIP, 2 * pitch), jnp.bfloat16),
            pltpu.SemaphoreType.DMA((4,)),
            pltpu.SemaphoreType.DMA((steps,)),
        ],
        compiler_params=pltpu.CompilerParams(vmem_limit_bytes=48 << 20),
    )(*points, by_pair)


def table_kernel(
    level_ref, filled_ref, omega_ref, bose_ref, vector_ref, ek_ref, ok_ref,
    absorb_ref, count_ref, turned_ref, pick_ref,
):
    f32 = jnp.float32
    points = level_ref.shape[0]
    q_local = omega_ref.shape[0]
    n = lax.broadcasted_iota(jnp.int32, (NB, NB), 0)
    at = lax.broadcasted_iota(jnp.int32, (NB, NB), 1)
    order = (n == (at % 8) * (NB // 8) + at // 8).astype(f32).astype(jnp.bfloat16)
    level = jnp.transpose(level_ref[...])
    filled = jnp.transpose(filled_ref[...])
    scale = 1.0 / (SMEARING * math.sqrt(2.0 * math.pi))
    electron_scale = scale / (256 * NB)
    phonon_scale = scale / (16 * NB)
    for i in range(points):
        q, k = divmod(i, points // q_local)
        offset = ek_ref[k] - level[:, i : i + 1]
        f = filled[:, i : i + 1]
        w = omega_ref[q : q + 1, :]
        n = bose_ref[q : q + 1, :]
        up = jnp.exp(-0.5 * ((offset + w) / SMEARING) ** 2)
        down = jnp.exp(-0.5 * ((offset - w) / SMEARING) ** 2)
        absorb_ref[i] = ((n + f) * up + (n + 1.0 - f) * down) * electron_scale
        count_ref[i] = (ok_ref[k] - f) * up * phonon_scale
        for part in range(2):
            turned_ref[i, part * NB : (part + 1) * NB, :] = small_dot(
                vector_ref[i, part], order, ((0,), (0,))
            ).astype(jnp.bfloat16)
    lane = lax.broadcasted_iota(jnp.int32, pick_ref.shape, 0)
    col = lax.broadcasted_iota(jnp.int32, pick_ref.shape, 1)
    place = col % LANES
    wanted = (place // STRIP) * LANES + (place % STRIP) * PARTS + col // LANES
    pick_ref[...] = (lane == wanted).astype(f32).astype(jnp.bfloat16)


def tables(levels, filled, frequencies, bose, vectors, energy_k, occupation_k, width):
    q_local, k_local, bands = levels.shape
    points = q_local * k_local
    modes = frequencies.shape[1]
    vmem = pl.BlockSpec(memory_space=pltpu.VMEM)
    smem = pl.BlockSpec(memory_space=pltpu.SMEM)
    weight = jax.ShapeDtypeStruct((points, bands, modes), jnp.float32)
    return pl.pallas_call(
        table_kernel,
        in_specs=[vmem] * 5 + [smem] * 2,
        out_specs=[vmem] * 4,
        out_shape=[
            weight,
            weight,
            jax.ShapeDtypeStruct((points, 2 * bands, bands), jnp.bfloat16),
            jax.ShapeDtypeStruct((width, PARTS * LANES), jnp.bfloat16),
        ],
        compiler_params=pltpu.CompilerParams(vmem_limit_bytes=48 << 20),
    )(
        levels.reshape(points, bands),
        filled.reshape(points, bands),
        frequencies,
        bose,
        vectors.reshape(points, 2, bands, bands),
        energy_k,
        occupation_k,
    )


def width_kernel(
    block_ref, modes_ref, turned_ref, absorb_ref, count_ref, pick_ref,
    copies_ref, phonon_ref, spread, cycle, moded,
):
    f32 = jnp.float32
    bf16 = jnp.bfloat16
    q_local = modes_ref.shape[0]
    k_local = PARTS // 2
    rows = block_ref.shape[0]
    per_source = 75
    depth = 80
    sources = rows // q_local
    phases = 8
    runs = sources // phases
    to = lax.broadcasted_iota(jnp.int32, (rows, rows), 0)
    source = lax.broadcasted_iota(jnp.int32, (rows, rows), 1)
    wanted = (to % runs) * (phases * q_local) + (to // runs) % phases * q_local
    wanted = wanted + to // (runs * phases)
    order = (source == wanted).astype(f32).astype(bf16)
    block = jnp.dot(order, block_ref[...], preferred_element_type=f32).astype(bf16)
    for part in range(0, PARTS, 2):
        two = jnp.dot(
            block, pick_ref[:, part * LANES : (part + 2) * LANES], preferred_element_type=f32
        )
        spread[part] = two[:, :LANES]
        spread[part + 1] = two[:, LANES:]
    electron = [None] * k_local
    for q in range(q_local):
        for part in range(2):
            m = modes_ref[q, part].astype(f32)
            cycle[q, 0:MODES, part * LANES : part * LANES + MODES] = m
            cycle[q, MODES : 2 * MODES, part * LANES : part * LANES + MODES] = m
        sums = [None] * 5
        for phase in range(phases):
            start = (per_source * phase) % MODES
            first = (per_source * phase) // MODES
            left = jnp.concatenate(
                [
                    spread[part, (q * phases + phase) * runs : (q * phases + phase + 1) * runs, :]
                    for part in range(PARTS)
                ],
                axis=0,
            )[:, :depth].astype(bf16)
            right = cycle[q, pl.ds(start, depth), :]
            at = lax.broadcasted_iota(jnp.int32, right.shape, 0)
            until = min(MODES - start, per_source)
            pieces = [(first, jnp.where(at < until, right, 0.0))]
            if until < per_source:
                pieces.append(
                    (first + 1, jnp.where((at >= until) & (at < per_source), right, 0.0))
                )
            for n, piece in pieces:
                value = jnp.dot(left, piece.astype(bf16), preferred_element_type=f32)
                sums[n] = value if sums[n] is None else sums[n] + value
        half = PARTS // 2 * runs
        for n in range(5):
            real = sums[n][:half, :LANES] - sums[n][half:, LANES:]
            imag = sums[n][:half, LANES:] + sums[n][half:, :LANES]
            for k in range(k_local):
                moded[q * k_local + k, 0, n * runs : (n + 1) * runs, :] = real[k * runs : (k + 1) * runs]
                moded[q * k_local + k, 1, n * runs : (n + 1) * runs, :] = imag[k * runs : (k + 1) * runs]
        phonon = None
        for k in range(k_local):
            i = q * k_local + k
            right = jnp.concatenate([moded[i, 0], moded[i, 1]], axis=1).astype(bf16)
            both = jnp.dot(turned_ref[i], right, preferred_element_type=f32)
            real = both[:NB, :MODES] + both[NB:, LANES : LANES + MODES]
            imag = both[:NB, LANES : LANES + MODES] - both[NB:, :MODES]
            weight = real * real + imag * imag
            value = jnp.sum(weight * absorb_ref[i], axis=0, keepdims=True)
            electron[k] = value if electron[k] is None else electron[k] + value
            value = jnp.sum(weight * count_ref[i], axis=0, keepdims=True)
            phonon = value if phonon is None else phonon + value
        phonon_ref[q : q + 1, :] = phonon
    copies_ref[...] = jnp.broadcast_to(jnp.concatenate(electron, axis=0)[None], copies_ref.shape)


def widths(block, phonon_modes, turned, absorb, count, pick, members):
    q_local, _, modes, _ = phonon_modes.shape
    rows = block.shape[0]
    vmem = pl.BlockSpec(memory_space=pltpu.VMEM)
    return pl.pallas_call(
        width_kernel,
        in_specs=[vmem] * 6,
        out_specs=[vmem] * 2,
        out_shape=[
            jax.ShapeDtypeStruct((members, PARTS // 2, modes), jnp.float32),
            jax.ShapeDtypeStruct((q_local, modes), jnp.float32),
        ],
        scratch_shapes=[
            pltpu.VMEM((PARTS, rows, LANES), jnp.float32),
            pltpu.VMEM((q_local, 2 * modes, 2 * LANES), jnp.float32),
            pltpu.VMEM((q_local * PARTS // 2, 2, NB, LANES), jnp.float32),
        ],
        compiler_params=pltpu.CompilerParams(vmem_limit_bytes=48 << 20),
    )(block, phonon_modes, turned, absorb, count, pick)


def added(*arrays):
    return sum(a.astype(jnp.float32) for a in arrays).astype(jnp.bfloat16)


def on_device(
    coupling,
    kpoints,
    qpoints,
    electron_cells,
    phonon_cells,
    phonon_modes,
    band_vectors,
    energies_kq,
    occupations_kq,
    energy_k,
    occupation_k,
    frequencies,
    bose_factors,
):
    q_local = frequencies.shape[0]
    members = lax.axis_size("ka")
    beside = [(i, i ^ 1) for i in range(members)]
    across = [(i, i ^ 2) for i in range(members)]
    near_keep, near_send, far_keep, far_send = products(
        kpoints, qpoints, electron_cells, phonon_cells, coupling
    )
    q_total, width = far_send.shape
    chip = added(far_keep, lax.ppermute(far_send, "ka", beside))
    chip, energy_k = lax.optimization_barrier((chip, energy_k))
    theirs = lax.ppermute(chip, "ka", across)
    prepared = tables(
        energies_kq,
        occupations_kq,
        frequencies,
        bose_factors,
        band_vectors,
        energy_k,
        occupation_k,
        width,
    )
    near_send, prepared = lax.optimization_barrier((near_send, prepared))
    near = lax.ppermute(near_send, "ka", beside)
    chunks = added(near_keep, near, theirs).reshape(q_total // q_local, q_local, width)
    chunks, prepared, phonon_modes = lax.optimization_barrier((chunks, prepared, phonon_modes))
    arrived = lax.all_to_all(chunks, "pb", 0, 0, tiled=True)
    absorb, count, turned, pick = prepared
    copies, phonon = widths(
        arrived.reshape(q_total, width),
        phonon_modes,
        turned,
        absorb,
        count,
        pick,
        q_total // q_local,
    )
    phonons = [phonon] + [
        lax.ppermute(phonon, "ka", [(i, i ^ flip) for i in range(members)])
        for flip in range(1, members)
    ]
    electrons = lax.all_to_all(copies, "pb", 0, 0, tiled=True)
    return (electrons.sum(axis=0), (phonons[0] + phonons[1]) + (phonons[2] + phonons[3]))


def solution(mesh):
    in_specs = (
        P(None, "ka", "pb", None),
        P(),
        P(),
        P(),
        P(),
        P("pb", None, None, None),
        P("pb", "ka", None, None, None),
        P("pb", "ka", None),
        P("pb", "ka", None),
        P("ka"),
        P("ka"),
        P("pb", None),
        P("pb", None),
    )
    out_specs = (P("ka", None), P("pb", None))
    return jax.shard_map(
        on_device, mesh=mesh, in_specs=in_specs, out_specs=out_specs, check_vma=False
    )
```

```python
import math

import jax
import jax.numpy as jnp
from jax import lax
from jax.experimental import pallas as pl
from jax.experimental.pallas import tpu as pltpu
from jax.sharding import PartitionSpec as P

NB = 40
MODES = 120
NG = 100
SMEARING = 0.05

STRIP = 16
LANES = 128
PARTS = 8


def whole_turn_cosine(ticks):
    rest = ticks - NG * jnp.floor((ticks + 0.5) * (1.0 / NG))
    y = (jnp.abs(rest - NG // 2) - NG // 4) * (2.0 * math.pi / NG)
    z = y * y
    series = -1.0 / 39916800.0
    for term in (1.0 / 362880.0, -1.0 / 5040.0, 1.0 / 120.0, -1.0 / 6.0, 1.0):
        series = series * z + term
    return y * series


def small_dot(left, right, dims):
    return lax.dot_general(left, right, (dims, ((), ())), preferred_element_type=jnp.float32)


def product_kernel(
    kpt_hbm, qpt_hbm, ecell_hbm, pcell_hbm, g_hbm, near_keep, near_send, far_keep, far_send,
    kpt_ref, qpt_ref, ecell_ref, pcell_ref, g_ref, table, rows, small_sem, strip_sem,
):
    q_total = qpt_ref.shape[1]
    cells = g_ref.shape[2]
    pairs = g_hbm.shape[1]
    phonons = g_hbm.shape[3]
    groups = kpt_ref.shape[1] // 4
    pitch = table.shape[1] // 2
    f32 = jnp.float32
    bf16 = jnp.bfloat16
    small = [
        pltpu.make_async_copy(source, target, small_sem.at[i])
        for i, (source, target) in enumerate(
            ((kpt_hbm, kpt_ref), (ecell_hbm, ecell_ref), (qpt_hbm, qpt_ref), (pcell_hbm, pcell_ref))
        )
    ]
    for copy in small:
        copy.start()
    strips = []
    for first in range(0, pairs, STRIP):
        part = pl.ds(first, min(STRIP, pairs - first))
        strips.append(
            pltpu.make_async_copy(g_hbm.at[:, part], g_ref.at[:, part], strip_sem.at[len(strips)])
        )
    strips[0].start()
    blank = jnp.zeros((table.shape[0], pitch - phonons), bf16)
    for part in range(2):
        table[:, part * pitch + phonons : (part + 1) * pitch] = blank
        for slot in range(2):
            for g in range(0, rows.shape[1], table.shape[0]):
                rows[slot, g : g + table.shape[0], part * pitch + phonons : (part + 1) * pitch] = blank
    for copy in small:
        copy.wait()
    for strip in strips[1:]:
        strip.start()
    mine = lax.axis_index("ka")
    kpt = kpt_ref[...].astype(f32).astype(bf16)
    qpt = qpt_ref[...].astype(f32).astype(bf16)
    ecell = ecell_ref[...].astype(f32).astype(bf16)
    pcell = pcell_ref[...].astype(f32).astype(bf16)
    height = 2 * PARTS * groups
    source = lax.broadcasted_iota(jnp.int32, (kpt.shape[1], height), 0)
    row = lax.broadcasted_iota(jnp.int32, (kpt.shape[1], height), 1)
    wanted = jnp.bitwise_xor((row // PARTS) % groups, mine) * 4 + row % 4
    k_rows = small_dot(kpt, (source == wanted).astype(f32).astype(bf16), ((1,), (0,)))
    source = lax.broadcasted_iota(jnp.int32, (ecell.shape[1], 2 * cells), 0)
    col = lax.broadcasted_iota(jnp.int32, (ecell.shape[1], 2 * cells), 1)
    wanted = mine * cells + jnp.where(col >= cells, col - cells, col)
    e_cols = small_dot(ecell, (source == wanted).astype(f32).astype(bf16), ((1,), (0,)))
    ticks = small_dot(k_rows.astype(bf16), e_cols.astype(bf16), ((0,), (0,)))
    row = lax.broadcasted_iota(jnp.int32, ticks.shape, 0)
    col = lax.broadcasted_iota(jnp.int32, ticks.shape, 1)
    turn = jnp.where(row >= height // 2, 25.0, 0.0)
    turn = turn - jnp.where(row % PARTS >= 4, 25.0, 0.0)
    turn = turn + jnp.where(col >= cells, 25.0, 0.0)
    mix = whole_turn_cosine(ticks + turn).astype(bf16)
    ticks = small_dot(qpt, pcell, ((0,), (0,)))
    table[:, 0:phonons] = whole_turn_cosine(ticks).astype(bf16)
    table[:, pitch : pitch + phonons] = whole_turn_cosine(ticks - 25.0).astype(bf16)

    def mixed_rows(s):
        values = []
        for j in range(STRIP):
            pair = s * STRIP + j
            if pair < pairs:
                both = jnp.concatenate([g_ref[0, pair], g_ref[1, pair]], axis=0)
                values.append(jnp.dot(mix, both, preferred_element_type=f32))
            else:
                values.append(jnp.zeros((height, phonons), f32))
            if j % 2 == 0:
                continue
            for set_ in range(2):
                for g in range(groups):
                    at = (set_ * groups + g) * PARTS
                    two = jnp.concatenate(
                        [values[j - 1][at : at + PARTS], values[j][at : at + PARTS]], axis=0
                    )
                    to = g * LANES + (j - 1) * PARTS
                    rows[s % 2, to : to + 2 * PARTS, set_ * pitch : set_ * pitch + phonons] = (
                        two.astype(bf16)
                    )

    def turned_rows(s):
        turned = small_dot(table[...], rows[s % 2], ((1,), (1,)))
        to = pl.ds(s * LANES, LANES)
        for g, ref in enumerate((near_keep, near_send, far_keep, far_send)):
            ref[:, to] = turned[:, g * LANES : (g + 1) * LANES].astype(bf16)

    for s, strip in enumerate(strips):
        strip.wait()
        mixed_rows(s)
        if s > 0:
            turned_rows(s - 1)
    turned_rows(len(strips) - 1)


def products(kpoints, qpoints, electron_cells, phonon_cells, coupling):
    parts, cells, pairs, phonons = coupling.shape
    k_total = kpoints.shape[1]
    q_total = qpoints.shape[1]
    steps = pl.cdiv(pairs, STRIP)
    pitch = pl.cdiv(phonons, LANES) * LANES
    by_pair = jnp.transpose(coupling, (0, 2, 1, 3))
    out = jax.ShapeDtypeStruct((q_total, steps * LANES), jnp.bfloat16)
    points = [
        pltpu.with_memory_space_constraint(a, pltpu.HBM)
        for a in (kpoints, qpoints, electron_cells, phonon_cells)
    ]
    return pl.pallas_call(
        product_kernel,
        in_specs=[pl.BlockSpec(memory_space=pltpu.HBM)] * 5,
        out_specs=[pl.BlockSpec(memory_space=pltpu.VMEM)] * 4,
        out_shape=[out] * 4,
        scratch_shapes=[pltpu.VMEM(a.shape, a.dtype) for a in points]
        + [
            pltpu.VMEM(by_pair.shape, by_pair.dtype),
            pltpu.VMEM((q_total, 2 * pitch), jnp.bfloat16),
            pltpu.VMEM((2, 2 * k_total * STRIP, 2 * pitch), jnp.bfloat16),
            pltpu.SemaphoreType.DMA((4,)),
            pltpu.SemaphoreType.DMA((steps,)),
        ],
        compiler_params=pltpu.CompilerParams(vmem_limit_bytes=48 << 20),
    )(*points, by_pair)


def table_kernel(
    level_ref, filled_ref, omega_ref, bose_ref, vector_ref, ek_ref, ok_ref,
    absorb_ref, count_ref, turned_ref, pick_ref,
):
    f32 = jnp.float32
    points = level_ref.shape[0]
    q_local = omega_ref.shape[0]
    n = lax.broadcasted_iota(jnp.int32, (NB, NB), 0)
    at = lax.broadcasted_iota(jnp.int32, (NB, NB), 1)
    order = (n == (at % 8) * (NB // 8) + at // 8).astype(f32).astype(jnp.bfloat16)
    level = jnp.transpose(level_ref[...])
    filled = jnp.transpose(filled_ref[...])
    scale = 1.0 / (SMEARING * math.sqrt(2.0 * math.pi))
    electron_scale = scale / (256 * NB)
    phonon_scale = scale / (16 * NB)
    for i in range(points):
        q, k = divmod(i, points // q_local)
        offset = ek_ref[k] - level[:, i : i + 1]
        f = filled[:, i : i + 1]
        w = omega_ref[q : q + 1, :]
        n = bose_ref[q : q + 1, :]
        up = jnp.exp(-0.5 * ((offset + w) / SMEARING) ** 2)
        down = jnp.exp(-0.5 * ((offset - w) / SMEARING) ** 2)
        absorb_ref[i] = ((n + f) * up + (n + 1.0 - f) * down) * electron_scale
        count_ref[i] = (ok_ref[k] - f) * up * phonon_scale
        for part in range(2):
            turned_ref[i, part * NB : (part + 1) * NB, :] = small_dot(
                vector_ref[i, part], order, ((0,), (0,))
            ).astype(jnp.bfloat16)
    lane = lax.broadcasted_iota(jnp.int32, pick_ref.shape, 0)
    col = lax.broadcasted_iota(jnp.int32, pick_ref.shape, 1)
    place = col % LANES
    wanted = (place // STRIP) * LANES + (place % STRIP) * PARTS + col // LANES
    pick_ref[...] = (lane == wanted).astype(f32).astype(jnp.bfloat16)


def tables(levels, filled, frequencies, bose, vectors, energy_k, occupation_k, width):
    q_local, k_local, bands = levels.shape
    points = q_local * k_local
    modes = frequencies.shape[1]
    vmem = pl.BlockSpec(memory_space=pltpu.VMEM)
    smem = pl.BlockSpec(memory_space=pltpu.SMEM)
    weight = jax.ShapeDtypeStruct((points, bands, modes), jnp.float32)
    return pl.pallas_call(
        table_kernel,
        in_specs=[vmem] * 5 + [smem] * 2,
        out_specs=[vmem] * 4,
        out_shape=[
            weight,
            weight,
            jax.ShapeDtypeStruct((points, 2 * bands, bands), jnp.bfloat16),
            jax.ShapeDtypeStruct((width, PARTS * LANES), jnp.bfloat16),
        ],
        compiler_params=pltpu.CompilerParams(vmem_limit_bytes=48 << 20),
    )(
        levels.reshape(points, bands),
        filled.reshape(points, bands),
        frequencies,
        bose,
        vectors.reshape(points, 2, bands, bands),
        energy_k,
        occupation_k,
    )


def width_kernel(
    block_ref, modes_ref, turned_ref, absorb_ref, count_ref, pick_ref,
    copies_ref, phonon_ref, spread, cycle, moded,
):
    f32 = jnp.float32
    bf16 = jnp.bfloat16
    q_local = modes_ref.shape[0]
    k_local = PARTS // 2
    rows = block_ref.shape[0]
    per_source = 75
    depth = 80
    sources = rows // q_local
    phases = 8
    runs = sources // phases
    to = lax.broadcasted_iota(jnp.int32, (rows, rows), 0)
    source = lax.broadcasted_iota(jnp.int32, (rows, rows), 1)
    wanted = (to % runs) * (phases * q_local) + (to // runs) % phases * q_local
    wanted = wanted + to // (runs * phases)
    order = (source == wanted).astype(f32).astype(bf16)
    block = jnp.dot(order, block_ref[...], preferred_element_type=f32).astype(bf16)
    for part in range(0, PARTS, 2):
        two = jnp.dot(
            block, pick_ref[:, part * LANES : (part + 2) * LANES], preferred_element_type=f32
        )
        spread[part] = two[:, :LANES]
        spread[part + 1] = two[:, LANES:]
    electron = [None] * k_local
    for q in range(q_local):
        for part in range(2):
            m = modes_ref[q, part].astype(f32)
            cycle[q, 0:MODES, part * LANES : part * LANES + MODES] = m
            cycle[q, MODES : 2 * MODES, part * LANES : part * LANES + MODES] = m
        sums = [None] * 5
        for phase in range(phases):
            start = (per_source * phase) % MODES
            first = (per_source * phase) // MODES
            left = jnp.concatenate(
                [
                    spread[part, (q * phases + phase) * runs : (q * phases + phase + 1) * runs, :]
                    for part in range(PARTS)
                ],
                axis=0,
            )[:, :depth].astype(bf16)
            right = cycle[q, pl.ds(start, depth), :]
            at = lax.broadcasted_iota(jnp.int32, right.shape, 0)
            until = min(MODES - start, per_source)
            pieces = [(first, jnp.where(at < until, right, 0.0))]
            if until < per_source:
                pieces.append(
                    (first + 1, jnp.where((at >= until) & (at < per_source), right, 0.0))
                )
            for n, piece in pieces:
                value = jnp.dot(left, piece.astype(bf16), preferred_element_type=f32)
                sums[n] = value if sums[n] is None else sums[n] + value
        half = PARTS // 2 * runs
        for n in range(5):
            real = sums[n][:half, :LANES] - sums[n][half:, LANES:]
            imag = sums[n][:half, LANES:] + sums[n][half:, :LANES]
            for k in range(k_local):
                moded[q * k_local + k, 0, n * runs : (n + 1) * runs, :] = real[k * runs : (k + 1) * runs]
                moded[q * k_local + k, 1, n * runs : (n + 1) * runs, :] = imag[k * runs : (k + 1) * runs]
        phonon = None
        for k in range(k_local):
            i = q * k_local + k
            right = jnp.concatenate([moded[i, 0], moded[i, 1]], axis=1).astype(bf16)
            both = jnp.dot(turned_ref[i], right, preferred_element_type=f32)
            real = both[:NB, :MODES] + both[NB:, LANES : LANES + MODES]
            imag = both[:NB, LANES : LANES + MODES] - both[NB:, :MODES]
            weight = real * real + imag * imag
            value = jnp.sum(weight * absorb_ref[i], axis=0, keepdims=True)
            electron[k] = value if electron[k] is None else electron[k] + value
            value = jnp.sum(weight * count_ref[i], axis=0, keepdims=True)
            phonon = value if phonon is None else phonon + value
        phonon_ref[q : q + 1, :] = phonon
    copies_ref[...] = jnp.broadcast_to(jnp.concatenate(electron, axis=0)[None], copies_ref.shape)


def widths(block, phonon_modes, turned, absorb, count, pick, members):
    q_local, _, modes, _ = phonon_modes.shape
    rows = block.shape[0]
    vmem = pl.BlockSpec(memory_space=pltpu.VMEM)
    return pl.pallas_call(
        width_kernel,
        in_specs=[vmem] * 6,
        out_specs=[vmem] * 2,
        out_shape=[
            jax.ShapeDtypeStruct((members, PARTS // 2, modes), jnp.float32),
            jax.ShapeDtypeStruct((q_local, modes), jnp.float32),
        ],
        scratch_shapes=[
            pltpu.VMEM((PARTS, rows, LANES), jnp.float32),
            pltpu.VMEM((q_local, 2 * modes, 2 * LANES), jnp.float32),
            pltpu.VMEM((q_local * PARTS // 2, 2, NB, LANES), jnp.float32),
        ],
        compiler_params=pltpu.CompilerParams(vmem_limit_bytes=48 << 20),
    )(block, phonon_modes, turned, absorb, count, pick)


def added(*arrays):
    return sum(a.astype(jnp.float32) for a in arrays).astype(jnp.bfloat16)


def on_device(
    coupling,
    kpoints,
    qpoints,
    electron_cells,
    phonon_cells,
    phonon_modes,
    band_vectors,
    energies_kq,
    occupations_kq,
    energy_k,
    occupation_k,
    frequencies,
    bose_factors,
):
    q_local = frequencies.shape[0]
    members = lax.axis_size("ka")
    beside = [(i, i ^ 1) for i in range(members)]
    across = [(i, i ^ 2) for i in range(members)]
    near_keep, near_send, far_keep, far_send = products(
        kpoints, qpoints, electron_cells, phonon_cells, coupling
    )
    q_total, width = far_send.shape
    chip = added(far_keep, lax.ppermute(far_send, "ka", beside))
    chip, energy_k = lax.optimization_barrier((chip, energy_k))
    theirs = lax.ppermute(chip, "ka", across)
    prepared = tables(
        energies_kq,
        occupations_kq,
        frequencies,
        bose_factors,
        band_vectors,
        energy_k,
        occupation_k,
        width,
    )
    near_send, prepared = lax.optimization_barrier((near_send, prepared))
    near = lax.ppermute(near_send, "ka", beside)
    chunks = added(near_keep, near, theirs).reshape(q_total // q_local, q_local, width)
    chunks, prepared, phonon_modes = lax.optimization_barrier((chunks, prepared, phonon_modes))
    arrived = lax.all_to_all(chunks, "pb", 0, 0, tiled=True)
    absorb, count, turned, pick = prepared
    copies, phonon = widths(
        arrived.reshape(q_total, width),
        phonon_modes,
        turned,
        absorb,
        count,
        pick,
        q_total // q_local,
    )
    phonons = [phonon] + [
        lax.ppermute(phonon, "ka", [(i, i ^ flip) for i in range(members)])
        for flip in range(1, members)
    ]
    electrons = lax.all_to_all(copies, "pb", 0, 0, tiled=True)
    return (electrons.sum(axis=0), (phonons[0] + phonons[1]) + (phonons[2] + phonons[3]))


def solution(mesh):
    in_specs = (
        P(None, "ka", "pb", None),
        P(),
        P(),
        P(),
        P(),
        P("pb", None, None, None),
        P("pb", "ka", None, None, None),
        P("pb", "ka", None),
        P("pb", "ka", None),
        P("ka"),
        P("ka"),
        P("pb", None),
        P("pb", None),
    )
    out_specs = (P("ka", None), P("pb", None))
    return jax.shard_map(
        on_device, mesh=mesh, in_specs=in_specs, out_specs=out_specs, check_vma=False
    )
```

```python
import math

import jax
import jax.numpy as jnp
from jax import lax
from jax.experimental import pallas as pl
from jax.experimental.pallas import tpu as pltpu
from jax.sharding import PartitionSpec as P

NB = 40
MODES = 120
NG = 100
SMEARING = 0.05

STRIP = 16
LANES = 128
PARTS = 8


def whole_turn_cosine(ticks):
    rest = ticks - NG * jnp.floor((ticks + 0.5) * (1.0 / NG))
    y = (jnp.abs(rest - NG // 2) - NG // 4) * (2.0 * math.pi / NG)
    z = y * y
    series = -1.0 / 39916800.0
    for term in (1.0 / 362880.0, -1.0 / 5040.0, 1.0 / 120.0, -1.0 / 6.0, 1.0):
        series = series * z + term
    return y * series


def small_dot(left, right, dims):
    return lax.dot_general(left, right, (dims, ((), ())), preferred_element_type=jnp.float32)


def product_kernel(
    kpt_hbm, qpt_hbm, ecell_hbm, pcell_hbm, g_hbm, near_keep, near_send, far_keep, far_send,
    kpt_ref, qpt_ref, ecell_ref, pcell_ref, g_ref, table, rows, small_sem, strip_sem,
):
    q_total = qpt_ref.shape[1]
    cells = g_ref.shape[2]
    pairs = g_hbm.shape[1]
    phonons = g_hbm.shape[3]
    groups = kpt_ref.shape[1] // 4
    pitch = table.shape[1] // 2
    f32 = jnp.float32
    bf16 = jnp.bfloat16
    small = [
        pltpu.make_async_copy(source, target, small_sem.at[i])
        for i, (source, target) in enumerate(
            ((kpt_hbm, kpt_ref), (ecell_hbm, ecell_ref), (qpt_hbm, qpt_ref), (pcell_hbm, pcell_ref))
        )
    ]
    for copy in small:
        copy.start()
    strips = []
    for first in range(0, pairs, STRIP):
        part = pl.ds(first, min(STRIP, pairs - first))
        strips.append(
            pltpu.make_async_copy(g_hbm.at[:, part], g_ref.at[:, part], strip_sem.at[len(strips)])
        )
    strips[0].start()
    blank = jnp.zeros((table.shape[0], pitch - phonons), bf16)
    for part in range(2):
        table[:, part * pitch + phonons : (part + 1) * pitch] = blank
        for slot in range(2):
            for g in range(0, rows.shape[1], table.shape[0]):
                rows[slot, g : g + table.shape[0], part * pitch + phonons : (part + 1) * pitch] = blank
    for copy in small:
        copy.wait()
    for strip in strips[1:]:
        strip.start()
    mine = lax.axis_index("ka")
    kpt = kpt_ref[...].astype(f32).astype(bf16)
    qpt = qpt_ref[...].astype(f32).astype(bf16)
    ecell = ecell_ref[...].astype(f32).astype(bf16)
    pcell = pcell_ref[...].astype(f32).astype(bf16)
    height = 2 * PARTS * groups
    source = lax.broadcasted_iota(jnp.int32, (kpt.shape[1], height), 0)
    row = lax.broadcasted_iota(jnp.int32, (kpt.shape[1], height), 1)
    wanted = jnp.bitwise_xor((row // PARTS) % groups, mine) * 4 + row % 4
    k_rows = small_dot(kpt, (source == wanted).astype(f32).astype(bf16), ((1,), (0,)))
    source = lax.broadcasted_iota(jnp.int32, (ecell.shape[1], 2 * cells), 0)
    col = lax.broadcasted_iota(jnp.int32, (ecell.shape[1], 2 * cells), 1)
    wanted = mine * cells + jnp.where(col >= cells, col - cells, col)
    e_cols = small_dot(ecell, (source == wanted).astype(f32).astype(bf16), ((1,), (0,)))
    ticks = small_dot(k_rows.astype(bf16), e_cols.astype(bf16), ((0,), (0,)))
    row = lax.broadcasted_iota(jnp.int32, ticks.shape, 0)
    col = lax.broadcasted_iota(jnp.int32, ticks.shape, 1)
    turn = jnp.where(row >= height // 2, 25.0, 0.0)
    turn = turn - jnp.where(row % PARTS >= 4, 25.0, 0.0)
    turn = turn + jnp.where(col >= cells, 25.0, 0.0)
    mix = whole_turn_cosine(ticks + turn).astype(bf16)
    ticks = small_dot(qpt, pcell, ((0,), (0,)))
    table[:, 0:phonons] = whole_turn_cosine(ticks).astype(bf16)
    table[:, pitch : pitch + phonons] = whole_turn_cosine(ticks - 25.0).astype(bf16)

    def mixed_rows(s):
        values = []
        for j in range(STRIP):
            pair = s * STRIP + j
            if pair < pairs:
                both = jnp.concatenate([g_ref[0, pair], g_ref[1, pair]], axis=0)
                values.append(jnp.dot(mix, both, preferred_element_type=f32))
            else:
                values.append(jnp.zeros((height, phonons), f32))
            if j % 2 == 0:
                continue
            for set_ in range(2):
                for g in range(groups):
                    at = (set_ * groups + g) * PARTS
                    two = jnp.concatenate(
                        [values[j - 1][at : at + PARTS], values[j][at : at + PARTS]], axis=0
                    )
                    to = g * LANES + (j - 1) * PARTS
                    rows[s % 2, to : to + 2 * PARTS, set_ * pitch : set_ * pitch + phonons] = (
                        two.astype(bf16)
                    )

    def turned_rows(s):
        turned = small_dot(table[...], rows[s % 2], ((1,), (1,)))
        to = pl.ds(s * LANES, LANES)
        for g, ref in enumerate((near_keep, near_send, far_keep, far_send)):
            ref[:, to] = turned[:, g * LANES : (g + 1) * LANES].astype(bf16)

    for s, strip in enumerate(strips):
        strip.wait()
        mixed_rows(s)
        if s > 0:
            turned_rows(s - 1)
    turned_rows(len(strips) - 1)


def products(kpoints, qpoints, electron_cells, phonon_cells, coupling):
    parts, cells, pairs, phonons = coupling.shape
    k_total = kpoints.shape[1]
    q_total = qpoints.shape[1]
    steps = pl.cdiv(pairs, STRIP)
    pitch = pl.cdiv(phonons, LANES) * LANES
    by_pair = jnp.transpose(coupling, (0, 2, 1, 3))
    out = jax.ShapeDtypeStruct((q_total, steps * LANES), jnp.bfloat16)
    points = [
        pltpu.with_memory_space_constraint(a, pltpu.HBM)
        for a in (kpoints, qpoints, electron_cells, phonon_cells)
    ]
    return pl.pallas_call(
        product_kernel,
        in_specs=[pl.BlockSpec(memory_space=pltpu.HBM)] * 5,
        out_specs=[pl.BlockSpec(memory_space=pltpu.VMEM)] * 4,
        out_shape=[out] * 4,
        scratch_shapes=[pltpu.VMEM(a.shape, a.dtype) for a in points]
        + [
            pltpu.VMEM(by_pair.shape, by_pair.dtype),
            pltpu.VMEM((q_total, 2 * pitch), jnp.bfloat16),
            pltpu.VMEM((2, 2 * k_total * STRIP, 2 * pitch), jnp.bfloat16),
            pltpu.SemaphoreType.DMA((4,)),
            pltpu.SemaphoreType.DMA((steps,)),
        ],
        compiler_params=pltpu.CompilerParams(vmem_limit_bytes=48 << 20),
    )(*points, by_pair)


def table_kernel(
    level_ref, filled_ref, omega_ref, bose_ref, vector_ref, ek_ref, ok_ref,
    absorb_ref, count_ref, turned_ref, pick_ref, order_ref,
):
    f32 = jnp.float32
    points = level_ref.shape[0]
    q_local = omega_ref.shape[0]
    n = lax.broadcasted_iota(jnp.int32, (NB, NB), 0)
    at = lax.broadcasted_iota(jnp.int32, (NB, NB), 1)
    order = (n == (at % 8) * (NB // 8) + at // 8).astype(f32).astype(jnp.bfloat16)
    level = jnp.transpose(level_ref[...])
    filled = jnp.transpose(filled_ref[...])
    scale = 1.0 / (SMEARING * math.sqrt(2.0 * math.pi))
    electron_scale = scale / (256 * NB)
    phonon_scale = scale / (16 * NB)
    for i in range(points):
        q, k = divmod(i, points // q_local)
        offset = ek_ref[k] - level[:, i : i + 1]
        f = filled[:, i : i + 1]
        w = omega_ref[q : q + 1, :]
        n = bose_ref[q : q + 1, :]
        up = jnp.exp(-0.5 * ((offset + w) / SMEARING) ** 2)
        down = jnp.exp(-0.5 * ((offset - w) / SMEARING) ** 2)
        absorb_ref[i] = ((n + f) * up + (n + 1.0 - f) * down) * electron_scale
        count_ref[i] = (ok_ref[k] - f) * up * phonon_scale
        for part in range(2):
            turned_ref[i, part * NB : (part + 1) * NB, :] = small_dot(
                vector_ref[i, part], order, ((0,), (0,))
            ).astype(jnp.bfloat16)
    lane = lax.broadcasted_iota(jnp.int32, pick_ref.shape, 0)
    col = lax.broadcasted_iota(jnp.int32, pick_ref.shape, 1)
    place = col % LANES
    wanted = (place // STRIP) * LANES + (place % STRIP) * PARTS + col // LANES
    pick_ref[...] = (lane == wanted).astype(f32).astype(jnp.bfloat16)
    rows = order_ref.shape[0]
    phases = 8
    runs = rows // q_local // phases
    to = lax.broadcasted_iota(jnp.int32, (rows, rows), 0)
    source = lax.broadcasted_iota(jnp.int32, (rows, rows), 1)
    wanted = (to % runs) * (phases * q_local) + (to // runs) % phases * q_local
    wanted = wanted + to // (runs * phases)
    order_ref[...] = (source == wanted).astype(f32).astype(jnp.bfloat16)


def tables(levels, filled, frequencies, bose, vectors, energy_k, occupation_k, width, q_total):
    q_local, k_local, bands = levels.shape
    points = q_local * k_local
    modes = frequencies.shape[1]
    vmem = pl.BlockSpec(memory_space=pltpu.VMEM)
    smem = pl.BlockSpec(memory_space=pltpu.SMEM)
    weight = jax.ShapeDtypeStruct((points, bands, modes), jnp.float32)
    return pl.pallas_call(
        table_kernel,
        in_specs=[vmem] * 5 + [smem] * 2,
        out_specs=[vmem] * 5,
        out_shape=[
            weight,
            weight,
            jax.ShapeDtypeStruct((points, 2 * bands, bands), jnp.bfloat16),
            jax.ShapeDtypeStruct((width, PARTS * LANES), jnp.bfloat16),
            jax.ShapeDtypeStruct((q_total, q_total), jnp.bfloat16),
        ],
        compiler_params=pltpu.CompilerParams(vmem_limit_bytes=48 << 20),
    )(
        levels.reshape(points, bands),
        filled.reshape(points, bands),
        frequencies,
        bose,
        vectors.reshape(points, 2, bands, bands),
        energy_k,
        occupation_k,
    )


def width_kernel(
    block_ref, modes_ref, turned_ref, absorb_ref, count_ref, pick_ref, order_ref,
    copies_ref, phonon_ref, spread, cycle, moded,
):
    f32 = jnp.float32
    bf16 = jnp.bfloat16
    q_local = modes_ref.shape[0]
    k_local = PARTS // 2
    rows = block_ref.shape[0]
    per_source = 75
    depth = 80
    sources = rows // q_local
    phases = 8
    runs = sources // phases
    block = jnp.dot(order_ref[...], block_ref[...], preferred_element_type=f32).astype(bf16)
    for part in range(0, PARTS, 2):
        two = jnp.dot(
            block, pick_ref[:, part * LANES : (part + 2) * LANES], preferred_element_type=f32
        )
        spread[part] = two[:, :LANES]
        spread[part + 1] = two[:, LANES:]
    electron = [None] * k_local
    for q in range(q_local):
        for part in range(2):
            m = modes_ref[q, part].astype(f32)
            cycle[q, 0:MODES, part * LANES : part * LANES + MODES] = m
            cycle[q, MODES : 2 * MODES, part * LANES : part * LANES + MODES] = m
        sums = [None] * 5
        for phase in range(phases):
            start = (per_source * phase) % MODES
            first = (per_source * phase) // MODES
            left = jnp.concatenate(
                [
                    spread[part, (q * phases + phase) * runs : (q * phases + phase + 1) * runs, :]
                    for part in range(PARTS)
                ],
                axis=0,
            )[:, :depth].astype(bf16)
            right = cycle[q, pl.ds(start, depth), :]
            at = lax.broadcasted_iota(jnp.int32, right.shape, 0)
            until = min(MODES - start, per_source)
            pieces = [(first, jnp.where(at < until, right, 0.0))]
            if until < per_source:
                pieces.append(
                    (first + 1, jnp.where((at >= until) & (at < per_source), right, 0.0))
                )
            for n, piece in pieces:
                value = jnp.dot(left, piece.astype(bf16), preferred_element_type=f32)
                sums[n] = value if sums[n] is None else sums[n] + value
        half = PARTS // 2 * runs
        for n in range(5):
            real = sums[n][:half, :LANES] - sums[n][half:, LANES:]
            imag = sums[n][:half, LANES:] + sums[n][half:, :LANES]
            for k in range(k_local):
                moded[q * k_local + k, 0, n * runs : (n + 1) * runs, :] = real[k * runs : (k + 1) * runs]
                moded[q * k_local + k, 1, n * runs : (n + 1) * runs, :] = imag[k * runs : (k + 1) * runs]
        phonon = None
        for k in range(k_local):
            i = q * k_local + k
            right = jnp.concatenate([moded[i, 0], moded[i, 1]], axis=1).astype(bf16)
            both = jnp.dot(turned_ref[i], right, preferred_element_type=f32)
            real = both[:NB, :MODES] + both[NB:, LANES : LANES + MODES]
            imag = both[:NB, LANES : LANES + MODES] - both[NB:, :MODES]
            weight = real * real + imag * imag
            value = jnp.sum(weight * absorb_ref[i], axis=0, keepdims=True)
            electron[k] = value if electron[k] is None else electron[k] + value
            value = jnp.sum(weight * count_ref[i], axis=0, keepdims=True)
            phonon = value if phonon is None else phonon + value
        phonon_ref[q : q + 1, :] = phonon
    copies_ref[...] = jnp.broadcast_to(jnp.concatenate(electron, axis=0)[None], copies_ref.shape)


def widths(block, phonon_modes, turned, absorb, count, pick, order, members):
    q_local, _, modes, _ = phonon_modes.shape
    rows = block.shape[0]
    vmem = pl.BlockSpec(memory_space=pltpu.VMEM)
    return pl.pallas_call(
        width_kernel,
        in_specs=[vmem] * 7,
        out_specs=[vmem] * 2,
        out_shape=[
            jax.ShapeDtypeStruct((members, PARTS // 2, modes), jnp.float32),
            jax.ShapeDtypeStruct((q_local, modes), jnp.float32),
        ],
        scratch_shapes=[
            pltpu.VMEM((PARTS, rows, LANES), jnp.float32),
            pltpu.VMEM((q_local, 2 * modes, 2 * LANES), jnp.float32),
            pltpu.VMEM((q_local * PARTS // 2, 2, NB, LANES), jnp.float32),
        ],
        compiler_params=pltpu.CompilerParams(vmem_limit_bytes=48 << 20),
    )(block, phonon_modes, turned, absorb, count, pick, order)


def added(*arrays):
    return sum(a.astype(jnp.float32) for a in arrays).astype(jnp.bfloat16)


def on_device(
    coupling,
    kpoints,
    qpoints,
    electron_cells,
    phonon_cells,
    phonon_modes,
    band_vectors,
    energies_kq,
    occupations_kq,
    energy_k,
    occupation_k,
    frequencies,
    bose_factors,
):
    q_local = frequencies.shape[0]
    members = lax.axis_size("ka")
    beside = [(i, i ^ 1) for i in range(members)]
    across = [(i, i ^ 2) for i in range(members)]
    near_keep, near_send, far_keep, far_send = products(
        kpoints, qpoints, electron_cells, phonon_cells, coupling
    )
    q_total, width = far_send.shape
    chip = added(far_keep, lax.ppermute(far_send, "ka", beside))
    chip, energy_k = lax.optimization_barrier((chip, energy_k))
    theirs = lax.ppermute(chip, "ka", across)
    prepared = tables(
        energies_kq,
        occupations_kq,
        frequencies,
        bose_factors,
        band_vectors,
        energy_k,
        occupation_k,
        width,
        q_total,
    )
    near_send, prepared = lax.optimization_barrier((near_send, prepared))
    near = lax.ppermute(near_send, "ka", beside)
    chunks = added(near_keep, near, theirs).reshape(q_total // q_local, q_local, width)
    chunks, prepared, phonon_modes = lax.optimization_barrier((chunks, prepared, phonon_modes))
    arrived = lax.all_to_all(chunks, "pb", 0, 0, tiled=True)
    absorb, count, turned, pick, order = prepared
    copies, phonon = widths(
        arrived.reshape(q_total, width),
        phonon_modes,
        turned,
        absorb,
        count,
        pick,
        order,
        q_total // q_local,
    )
    phonons = [phonon] + [
        lax.ppermute(phonon, "ka", [(i, i ^ flip) for i in range(members)])
        for flip in range(1, members)
    ]
    electrons = lax.all_to_all(copies, "pb", 0, 0, tiled=True)
    return (electrons.sum(axis=0), (phonons[0] + phonons[1]) + (phonons[2] + phonons[3]))


def solution(mesh):
    in_specs = (
        P(None, "ka", "pb", None),
        P(),
        P(),
        P(),
        P(),
        P("pb", None, None, None),
        P("pb", "ka", None, None, None),
        P("pb", "ka", None),
        P("pb", "ka", None),
        P("ka"),
        P("ka"),
        P("pb", None),
        P("pb", None),
    )
    out_specs = (P("ka", None), P("pb", None))
    return jax.shard_map(
        on_device, mesh=mesh, in_specs=in_specs, out_specs=out_specs, check_vma=False
    )
```
